768 devices in a mesh: dp: 48 (over z, y_hi), mp: 8 (over y_lo, x), phase: 2 (over core).
Axes of the slice: x: 4, y: 8 (y_hi: 4, y_lo: 2; y = y_hi * 2 + y_lo), z: 12, core: 2. Of those that a mesh axis runs over, the one named last changes fastest.
Arguments:
- item_owner: int32 [24576, 1], P('dp'), may hold values from 0 to 47; in each aligned block of 512 rows (0 to 511, 512 to 1023, ...) at most 18 rows name the same one
- item_row: int32 [24576], P('dp'), may hold values from 0 to 1023
- segments: int32 [48, 2, 256], P('dp'), may hold values from 0 to 31, never falling along the last dimension, each value on 1 to 128 neighbouring positions
- neighbors: int32 [48, 2, 256, 8], P('dp'), may hold values from 0 to 255
- table: bfloat16 [49152, 1024], P('dp'), may hold values from -6 to 6
- gains: bfloat16 [2, 1024], P('phase'), may hold values from 0.099609375 to 1.8984375
- w_in: bfloat16 [2, 1024, 4, 1024], P('phase', None, None, 'mp'), may hold values from -0.1875 to 0.1875
- w_out: bfloat16 [2, 1024, 1024], P('phase', 'mp'), may hold values from -0.1875 to 0.1875
- w_ctx: bfloat16 [1024, 1024], P(None, 'mp'), may hold values from -0.1875 to 0.1875
- ctx_bias: bfloat16 [1024], P('mp'), may hold values from -3 to 3
Outputs:
- user_states: bfloat16 [48, 2, 256, 1024], P('dp', 'phase')
- impression_context: bfloat16 [48, 2, 256, 1024], P('dp', 'phase', None, 'mp')
The draws below stay inside these ranges and needn't reach their ends.
Inputs may be any that keep to these rules, and one draw needn't show every extreme that they name: `item_owner`: among the rows of one index of dp, at most 18 name the same owner.
All inputs are finite; a program needn't handle non-finite values.
Results may differ from the reference program's by a relative error of at most 0.02.
Values may be sent and summed in bfloat16 or wider, within the bound.
A program may use at most 32 MiB of HBM per device.

```python
import math
import jax
import jax.numpy as jnp
import numpy as np
from jax import lax

D = 1024
H = 8
HD = 128
NBR = 8
MBS = 2
MB_ROWS = 256
IMP = 256
TABLE_DEV = 1024
ROWS_DEV = 512
CAP = 18
N_DP = 48
N_MP = 8


def plant(values, rng, smallest, largest):
    longest = values.shape.index(max(values.shape))
    spots = []
    for shift in (0, 1):
        where = [jax.random.randint(jax.random.fold_in(rng, axis), (), 0, length) for axis, length in enumerate(values.shape)]
        where[longest] = (where[longest] + shift) % values.shape[longest]
        spots.append(tuple(where))
    return values.at[spots[0]].set(smallest).at[spots[1]].set(largest)


def levels(rng, dims, shards, smallest, top_value):
    factor_of, own = 1.0, jax.random.fold_in(rng, 6)
    for axis_at, parts in shards:
        draws = jnp.exp(jax.random.uniform(jax.random.fold_in(own, axis_at), (parts,), jnp.float32, smallest / len(shards), top_value / len(shards)))
        factor_of = factor_of * jnp.repeat(draws, dims[axis_at] // parts).reshape([-1 if axis == axis_at else 1 for axis in range(len(dims))])
    return factor_of


def split_up(amount, total, bound, slope):
    loads = [(1 << 20) // math.isqrt(grade ** slope) + 1 for grade in range(2, amount + 1)]
    spare, holding = total - bound - (amount - 1), [1] * (amount - 1)
    while spare > 0:
        movable = [i for i in range(amount - 1) if holding[i] < bound]
        whole, left = sum([loads[i] for i in movable]), spare
        for i in movable:
            more = min(bound - holding[i], max(1, left * loads[i] // whole), spare)
            holding[i] = holding[i] + more
            spare = spare - more
    return np.array([bound] + holding)


def uneven_parts(rng, number_of, total, bound, slope):
    if number_of == 2:
        one = jax.random.randint(rng, (), max(1, total - bound), min(bound, total - 1) + 1)
        return jnp.stack([one, total - one])
    lengths = jnp.asarray(split_up(number_of, total, bound, slope), jnp.int32)
    pairs = (number_of - 1) // 2
    source_of, sink = lengths[1:1 + 2 * pairs:2], lengths[2:2 + 2 * pairs:2]
    room = jnp.minimum(source_of - 1, bound - sink)
    shifted = jax.random.randint(jax.random.fold_in(rng, 1), (pairs,), 0, 1 << 20) % (room + 1)
    lengths = lengths.at[1:1 + 2 * pairs:2].set(source_of - shifted).at[2:2 + 2 * pairs:2].set(sink + shifted)
    return lengths[jax.random.permutation(jax.random.fold_in(rng, 2), number_of)]


def routed_block(stream_key, own, number, rows, count, top, most, slope):
    ranking = jax.random.permutation(stream_key, count)
    crowded, common = shares(count, rows * top, most, slope, True), shares(count, rows * top, most, slope, False)
    places = jnp.arange(count)

    def named(lengths, rotation):
        used = int((lengths > 0).sum())
        fixed = max(1, used // 4)
        passed = fixed + (places - fixed + rotation * (used - fixed)) % max(1, count - fixed)
        return jnp.zeros((count,), jnp.int32).at[ranking[jnp.where(places < fixed, places, passed)]].set(jnp.asarray(lengths, jnp.int32))

    lengths = jnp.where(number % 4 == 0, named(crowded, number // 4), named(common, number - number // 4 - 1))
    mixed = jax.random.permutation(jax.random.fold_in(own, 3), count)
    giver, receiver = mixed[0:count // 2 * 2:2], mixed[1:count // 2 * 2:2]
    margin = jnp.minimum(lengths[giver] - 1, most - lengths[receiver]) // 2
    margin = jnp.where((giver == ranking[0]) | (receiver == ranking[0]) | (lengths[receiver] == 0), 0, jnp.maximum(margin, 0))
    passed = jax.random.randint(jax.random.fold_in(own, 4), (count // 2,), 0, 1 << 20) % (margin + 1)
    lengths = lengths.at[giver].add(-passed).at[receiver].add(passed)
    labels = jnp.searchsorted(jnp.cumsum(lengths), jnp.arange(rows * top), side="right").astype(jnp.int32)
    table = labels.reshape(top, rows).T
    table = table[jax.random.permutation(jax.random.fold_in(own, 1), rows)]
    rotation = jax.random.randint(jax.random.fold_in(own, 2), (rows, 1), 0, top)
    return jnp.take_along_axis(table, (jnp.arange(top)[None, :] + rotation) % top, axis=1)


def shares(amount, total, limit, lean, full):
    weights = [(1 << 20) // math.isqrt(grade ** lean) + 1 for grade in range(1, amount + 1)]
    largest = limit if full else min(limit, max(-(-total // amount), total * weights[0] // sum(weights)))
    least = 1 if total - largest >= amount - 1 else 0
    given, spare = [largest] + [least] * (amount - 1), total - largest - least * (amount - 1)
    while spare > 0:
        free = [i for i in range(1, amount) if given[i] < largest] or [i for i in range(1, amount) if given[i] < limit]
        pool, left = sum([weights[i] for i in free]), spare
        for i in free:
            more = min(limit - given[i], max(1, left * weights[i] // pool), spare)
            given[i] = given[i] + more
            spare = spare - more
    return np.array(given)


def noise(rng, extent, spread, limit, cuts=(), kind=jnp.bfloat16):
    values = jax.random.normal(rng, extent, jnp.float32) * spread
    if len(cuts) > 0:
        values = levels(rng, extent, cuts, -0.22, 0.18) * values
    return jnp.clip(values, min=-limit, max=limit).astype(kind)


def setup_inputs(seed: int = 0) -> dict:
    splits = jax.random.split(jax.random.key(seed), 11)
    item_owner_keys = jax.random.split(jax.random.fold_in(splits[0], 1), (N_DP * ROWS_DEV) // ROWS_DEV)
    item_owner_turns = jax.random.permutation(jax.random.fold_in(splits[0], 3), (N_DP * ROWS_DEV) // ROWS_DEV)
    item_owner = jax.vmap(lambda own, number: routed_block(jax.random.fold_in(splits[0], 2), own, number, ROWS_DEV, N_DP, 1, CAP, 2))(item_owner_keys, item_owner_turns).reshape((N_DP * ROWS_DEV, 1))
    item_row = plant(jax.random.randint(splits[1], (N_DP * ROWS_DEV,), 0, TABLE_DEV), jax.random.fold_in(splits[1], 1), 0, TABLE_DEV - 1).astype(jnp.int32)
    segments = jax.vmap(lambda own: jnp.searchsorted(jnp.cumsum(uneven_parts(own, MB_ROWS // 8, MB_ROWS, MB_ROWS // 2, 2)), jnp.arange(MB_ROWS), side="right"))(jax.random.split(splits[2], N_DP * MBS)).reshape((N_DP, MBS, MB_ROWS)).astype(jnp.int32)
    neighbors = plant(jax.random.randint(splits[3], (N_DP, MBS, IMP, NBR), 0, MB_ROWS), jax.random.fold_in(splits[3], 1), 0, MB_ROWS - 1).astype(jnp.int32)
    table = noise(splits[4], (N_DP * TABLE_DEV, D), 1.0, 6.0, ((0, 48),))
    gains = jnp.clip(1.0 + 0.18 * jax.random.normal(splits[5], (2, D), jnp.float32), 0.099609375, 1.8984375).astype(jnp.bfloat16)
    w_in = noise(splits[6], (2, D, 4, H * HD), D ** -0.5, 0.1875, ((0, 2), (3, 8)))
    w_out = noise(splits[7], (2, H * HD, D), (H * HD) ** -0.5, 0.1875, ((0, 2), (1, 8)))
    w_ctx = noise(splits[8], (D, D), D ** -0.5, 0.1875, ((1, 8),))
    ctx_bias = noise(splits[9], (D,), 0.5, 3.0, ((0, 8),))
    return {"item_owner": item_owner, "item_row": item_row, "segments": segments, "neighbors": neighbors, "table": table, "gains": gains, "w_in": w_in, "w_out": w_out, "w_ctx": w_ctx, "ctx_bias": ctx_bias}


norm_eps = 1e-06

def hstu_layer(acts, seg_ids, gain, w_proj, w_back):
    rows_n = acts.shape[0]
    acts_f = acts.astype(jnp.float32)
    inv_rms = lax.rsqrt(lax.optimization_barrier(jnp.mean(acts_f * acts_f, axis=-1, keepdims=True)) + norm_eps)
    normed = (acts_f * inv_rms * gain.astype(jnp.float32)).astype(jnp.bfloat16)
    projected = jnp.dot(normed, w_proj.reshape(D, 4 * H * HD), preferred_element_type=jnp.float32)
    projected = jax.nn.silu(projected).astype(jnp.bfloat16).reshape(rows_n, 4, H, HD)
    gates_u = projected[:, 0].astype(jnp.float32)
    values_h = projected[:, 1].astype(jnp.float32)
    queries = projected[:, 2].astype(jnp.float32)
    keys_h = projected[:, 3].astype(jnp.float32)
    scores = jnp.einsum('qhd,khd->hqk', queries, keys_h) * HD ** (-0.5)
    position = jnp.arange(rows_n)
    allowed = (position[None, :] <= position[:, None]) & (seg_ids[:, None] == seg_ids[None, :])
    weights = (jnp.where(allowed[None], jax.nn.silu(scores), 0.0) / MB_ROWS).astype(jnp.bfloat16)
    mixed = jnp.einsum('hqk,khd->qhd', weights.astype(jnp.float32), values_h)
    mixed = mixed * lax.rsqrt(lax.optimization_barrier(jnp.mean(mixed * mixed, axis=-1, keepdims=True)) + norm_eps)
    group_cols = H * HD // N_MP
    gated = (mixed * gates_u).astype(jnp.bfloat16).reshape(rows_n, N_MP, group_cols).astype(jnp.float32)
    partial_terms = jnp.einsum('rjc,jcd->jrd', gated, w_back.reshape(N_MP, group_cols, D).astype(jnp.float32))
    partial_terms = lax.optimization_barrier(partial_terms.astype(jnp.bfloat16)).astype(jnp.float32)
    return (acts_f + lax.optimization_barrier(jnp.sum(partial_terms, axis=0))).astype(jnp.bfloat16)

def context_score(states, neigh_rows, w_ctx, ctx_bias):
    picked = jnp.take(states, neigh_rows.reshape(-1), axis=0).astype(jnp.float32)
    context = lax.optimization_barrier(jnp.mean(picked.reshape(neigh_rows.shape[0], NBR, D), axis=1)).astype(jnp.bfloat16)
    summed = jnp.dot(context, w_ctx, preferred_element_type=jnp.float32) + ctx_bias.astype(jnp.float32)
    return jax.nn.silu(summed).astype(jnp.bfloat16)

def reference(item_owner, item_row, segments, neighbors, table, gains, w_in, w_out, w_ctx, ctx_bias):
    item_ids = (item_owner[:, 0] * TABLE_DEV + item_row).astype(jnp.int32)
    acts_all = jnp.take(table, item_ids, axis=0).reshape(N_DP, MBS, MB_ROWS, D)

    def one_batch(packed):
        acts_m, seg_m, neigh_m = packed
        first = hstu_layer(acts_m, seg_m, gains[0], w_in[0], w_out[0])
        second = hstu_layer(first, seg_m, gains[1], w_in[1], w_out[1])
        return (second, context_score(second, neigh_m, w_ctx, ctx_bias))

    def one_group(packed):
        return lax.map(one_batch, packed)
    return lax.map(one_group, (acts_all, segments, neighbors))
```

```python
import functools

import jax
import jax.numpy as jnp
from jax import lax
from jax.experimental import pallas as pl
from jax.experimental.pallas import tpu as pltpu
from jax.sharding import PartitionSpec as P

MESH = pl.DeviceIdType.MESH
F32 = jnp.float32
BF16 = jnp.bfloat16
I32 = jnp.int32

D = 1024
HD = 128
NBR = 8
ROWS = 256
MP = 8
ZN = 12
YN = 4
PEERS = ZN // 2 * YN
SLOTS = 32
OWN = ROWS // MP
EPS = 1e-06


def silu(x):
    half = 0.5 * x
    return half * (1.0 + jnp.tanh(half))


def iota(shape, axis):
    return lax.broadcasted_iota(I32, shape, axis)


def to_column(row):
    n = row.shape[1]
    diag = iota((n, n), 0) == iota((n, n), 1)
    return jnp.sum(jnp.where(diag, jnp.broadcast_to(row, (n, n)), 0.0), axis=1, keepdims=True)


def kernel(
    owner_ref, item_ref, seg_ref, nbr_ref, gain_ref, bias_ref, table_hbm, w_hbm, wo_hbm, wctx_hbm,
    out_hbm, ctx_ref,
    tcol, w4, wp, wo, wctx, gbuf, reqout, reqin, repout, repin, pick, part0, partin, xcols,
    mask, counts, nrm, part, rsin, xrow, states,
    loc, req_s, req_r, rep_s, rep_r, wex_s, wex_r, xp_s, xp_r, ag_s, ag_r, rs_s, rs_r, out_s,
):
    g = lax.axis_index("dp")
    m = lax.axis_index("mp")
    p = lax.axis_index("phase")
    q = 1 - p
    zg, yg = g // YN, g % YN
    slot_me = (zg // 2) * YN + yg
    is_even = p == 0

    def dp_peer(j, dy):
        z = lax.rem(zg + 2 * j + p, ZN)
        y = lax.rem(yg + dy, YN)
        return z * YN + y, (z // 2) * YN + y

    def mp_peer(d):
        return lax.rem(m + d, MP)

    def remote(src, dst, s, r, dev):
        return pltpu.make_async_remote_copy(
            src_ref=src, dst_ref=dst, send_sem=s, recv_sem=r, device_id=dev, device_id_type=MESH
        )

    def drain(ref, sem):
        pltpu.make_async_copy(ref, ref, sem).wait()

    barrier = pltpu.get_barrier_semaphore()

    def greet(dev):
        pl.semaphore_signal(barrier, inc=1, device_id=dev, device_id_type=MESH)

    far_first = (3, 2, 4, 1, 5, 0)
    for j in far_first:
        for dy in (2, 1, 3, 0):
            o, _ = dp_peer(j, dy)
            if (j, dy) == (0, 0):
                @pl.when(p == 1)
                def _():
                    greet((o, m, p))
            else:
                greet((o, m, p))
    for d in range(1, MP):
        greet((g, mp_peer(d), p))
    greet((g, m, q))

    col0 = pl.multiple_of(m * HD, HD)
    loads = [
        pltpu.make_async_copy(table_hbm.at[:, pl.ds(col0, HD)], tcol, loc.at[0]),
        pltpu.make_async_copy(w_hbm, w4.at[p], loc.at[1]),
        pltpu.make_async_copy(wo_hbm, wo.at[p], loc.at[2]),
        pltpu.make_async_copy(wctx_hbm, wctx, loc.at[3]),
    ]
    for load in loads:
        load.start()
    gbuf[p] = jnp.broadcast_to(gain_ref[...].astype(F32), (8, D))

    n_rows = owner_ref.shape[1]
    owners = owner_ref[...]
    items = item_ref[...]
    slot_col = iota((PEERS, n_rows), 0)
    owner_of_slot = (2 * (slot_col // YN) + lax.rem(zg + p, 2)) * YN + slot_col % YN
    hit = (jnp.broadcast_to(owners, (PEERS, n_rows)) == owner_of_slot).astype(F32)
    before = (iota((n_rows, n_rows), 0) < iota((n_rows, n_rows), 1)).astype(F32).astype(BF16)
    count = jnp.dot(hit.astype(BF16), before, preferred_element_type=F32)
    rank = jnp.sum(hit * count, axis=0, keepdims=True)
    mine = jnp.sum(hit, axis=0, keepdims=True)
    slot_row = jnp.sum(hit * slot_col.astype(F32), axis=0, keepdims=True)
    key = jnp.where(mine > 0.5, slot_row * SLOTS + rank, -1.0)
    ranked = jnp.where(mine > 0.5, rank, -1.0)
    at_rank = (iota((HD, n_rows), 0).astype(F32) == jnp.broadcast_to(ranked, (HD, n_rows)))
    at_rank = at_rank.astype(F32).astype(BF16)
    hi = (items >> 5).astype(F32)
    lo = (items & 31).astype(F32)
    both = jnp.concatenate([hit * hi, hit * lo], axis=0).astype(BF16)
    found = lax.dot_general(both, at_rank, (((1,), (1,)), ((), ())), preferred_element_type=F32)
    wanted = (found[:PEERS] * 32.0 + found[PEERS:]).astype(I32)
    for s in range(PEERS):
        reqout[s] = wanted[s : s + 1]

    pl.semaphore_wait(barrier, 31 + p)

    def to_peers(src_of, dst, s_sem, r_sem, js):
        for j in js:
            for dy in (2, 1, 3, 0):
                o, s = dp_peer(j, dy)
                if (j, dy) == (0, 0):
                    @pl.when(is_even)
                    def _():
                        pltpu.make_async_copy(src_of.at[s], dst.at[slot_me], r_sem).start()

                    @pl.when(p == 1)
                    def _():
                        remote(src_of.at[s], dst.at[slot_me], s_sem, r_sem, (o, m, p)).start()
                else:
                    remote(src_of.at[s], dst.at[slot_me], s_sem, r_sem, (o, m, p)).start()

    to_peers(reqout, reqin, req_s, req_r, far_first)

    loads[1].wait()
    loads[2].wait()
    sibling = (g, m, q)
    exchange = [
        remote(w4.at[p], w4.at[p], wex_s.at[0], wex_r.at[0], sibling),
        remote(wo.at[p], wo.at[p], wex_s.at[1], wex_r.at[1], sibling),
        remote(gbuf.at[p], gbuf.at[p], wex_s.at[2], wex_r.at[2], sibling),
    ]
    for copy in exchange:
        copy.start()

    per_chunk = 64
    src_col = iota((4 * per_chunk, 4 * per_chunk), 1)
    dst_row = iota((4 * per_chunk, 4 * per_chunk), 0)
    spread = (src_col == 4 * (dst_row % per_chunk) + dst_row // per_chunk).astype(F32).astype(BF16)

    def arrange(sec):
        def body(i, carry):
            base = pl.multiple_of(i * 4 * per_chunk, 4 * per_chunk)
            moved = jnp.dot(spread, w4[sec, pl.ds(base, 4 * per_chunk), :], preferred_element_type=F32)
            moved = moved.astype(BF16)
            to = pl.multiple_of(i * per_chunk, per_chunk)
            for c in range(4):
                wp[sec, pl.ds(to, per_chunk), c * HD : (c + 1) * HD] = moved[
                    c * per_chunk : (c + 1) * per_chunk
                ]
            return carry

        lax.fori_loop(0, D // per_chunk, body, 0)

    arrange(p)
    key_col = to_column(key)
    for h in range(2):
        lanes = iota((ROWS, PEERS * SLOTS), 1).astype(F32)
        pick[h] = (key_col[h * ROWS : (h + 1) * ROWS] == lanes).astype(F32).astype(BF16)

    loads[0].wait()
    drain(reqin, req_r)
    for pair in ((3, 2), (4, 1), (5, 0)):
        columns = []
        for j in pair:
            z = lax.rem(zg + 2 * j + p, ZN)
            base = (z // 2) * YN
            asked = jnp.broadcast_to(reqin[pl.ds(base, YN)], (YN, SLOTS, HD))
            on = iota((YN, SLOTS, HD), 1) == iota((YN, SLOTS, HD), 2)
            columns.append(
                jnp.sum(jnp.where(on, asked.astype(F32), 0.0), axis=2, keepdims=True).reshape(
                    YN * SLOTS, 1
                )
            )
        column = jnp.concatenate(columns, axis=0)
        size = 2 * YN * SLOTS
        hot = (column == iota((size, D), 1).astype(F32)).astype(F32).astype(BF16)
        rows = jnp.dot(hot, tcol[...], preferred_element_type=F32).astype(BF16)
        rows = rows.reshape(2, YN, SLOTS, HD)
        for i, j in enumerate(pair):
            z = lax.rem(zg + 2 * j + p, ZN)
            repout[pl.ds((z // 2) * YN, YN)] = rows[i]
        to_peers(repout, repin, rep_s, rep_r, pair)

    exchange[0].wait_recv()
    exchange[1].wait_recv()
    exchange[2].wait_recv()
    arrange(q)
    seg = seg_ref[pl.ds(p, 1), :].astype(F32)
    seg_col = to_column(seg)
    below = iota((ROWS, ROWS), 1) <= iota((ROWS, ROWS), 0)
    same = seg_col == jnp.broadcast_to(seg, (ROWS, ROWS))
    mask[...] = jnp.where(below & same, 1.0 / ROWS, 0.0)
    hits = jnp.zeros((ROWS, ROWS), F32)
    near = nbr_ref[p]
    for n in range(NBR):
        row = jnp.broadcast_to(near[n : n + 1], (ROWS, ROWS))
        hits = hits + jnp.where(row == iota((ROWS, ROWS), 0), 1.0 / NBR, 0.0)
    counts[...] = hits.T.astype(BF16)

    drain(repin, rep_r)
    for h in range(2):
        part0[h] = jnp.dot(
            pick[h], repin[...].reshape(PEERS * SLOTS, HD), preferred_element_type=F32
        ).astype(BF16)
    swap = remote(part0.at[q], partin, xp_s, xp_r, sibling)
    swap.start()
    swap.wait_recv()
    xcols[m] = part0[p] + partin[...]

    def to_group(src_of, dst, s_sem, r_of):
        for d in (4, 2, 6, 5, 7, 1, 3):
            to = mp_peer(d)
            remote(src_of(to), dst, s_sem, r_of, (g, to, p)).start()

    to_group(lambda to: xcols.at[m], xcols.at[m], ag_s.at[0], ag_r.at[0])
    drain(xcols.at[pl.ds(0, MP - 1)], ag_r.at[0])

    total = jnp.zeros((ROWS, 1), F32)
    for k in range(MP):
        block = xcols[k].astype(F32)
        total = total + jnp.sum(block * block, axis=1, keepdims=True)
    inv = lax.rsqrt(total * (1.0 / D) + EPS)
    for k in range(MP):
        scaled = xcols[k].astype(F32) * inv * gbuf[0, 0:1, k * HD : (k + 1) * HD]
        nrm[0, :, :, k * HD : (k + 1) * HD] = scaled.astype(BF16).reshape(MP, OWN, HD)
    own_row = pl.multiple_of(m * OWN, OWN)
    for k in range(MP):
        xrow[:, k * HD : (k + 1) * HD] = xcols[k, pl.ds(own_row, OWN), :].astype(F32)

    for sec in range(2):
        proj = jnp.dot(
            nrm[sec].reshape(ROWS, D), wp[sec], preferred_element_type=F32
        )
        proj = silu(proj).astype(BF16)
        gate, value = proj[:, :HD], proj[:, HD : 2 * HD]
        query, keys = proj[:, 2 * HD : 3 * HD], proj[:, 3 * HD :]
        scores = lax.dot_general(
            query, keys, (((1,), (1,)), ((), ())), preferred_element_type=F32
        ) * HD ** (-0.5)
        attn = (silu(scores) * mask[...]).astype(BF16)
        mixed = jnp.dot(attn, value, preferred_element_type=F32)
        mixed = mixed * lax.rsqrt(jnp.mean(mixed * mixed, axis=1, keepdims=True) + EPS)
        gated = (mixed * gate.astype(F32)).astype(BF16)
        back = jnp.dot(gated, wo[sec], preferred_element_type=F32).astype(BF16)
        part[sec] = back.reshape(MP, OWN, D)
        to_group(
            lambda to: part.at[sec, to], rsin.at[sec, m], rs_s.at[sec], rs_r.at[sec, m]
        )
        acc = part[sec, m].astype(F32)
        for d in (1, 3, 5, 7, 2, 6, 4):
            src = mp_peer(d)
            drain(rsin.at[sec, src], rs_r.at[sec, src])
            acc = acc + rsin[sec, src].astype(F32)
        new = (xrow[...] + acc).astype(BF16)
        if sec == 0:
            newf = new.astype(F32)
            xrow[...] = newf
            inv = lax.rsqrt(jnp.mean(newf * newf, axis=1, keepdims=True) + EPS)
            nrm[1, m] = (newf * inv * gbuf[1, 0:1, :]).astype(BF16)
            to_group(lambda to: nrm.at[1, m], nrm.at[1, m], ag_s.at[1], ag_r.at[1])
            drain(nrm.at[1, pl.ds(0, MP - 1)], ag_r.at[1])
        else:
            states[m] = new
            to_group(lambda to: states.at[m], states.at[m], ag_s.at[2], ag_r.at[2])
            drain(states.at[pl.ds(0, MP - 1)], ag_r.at[2])

    write = pltpu.make_async_copy(states, out_hbm, out_s)
    write.start()
    loads[3].wait()
    scored = jnp.dot(
        states[...].reshape(ROWS, D), wctx[...], preferred_element_type=F32
    ).astype(BF16)
    summed = jnp.dot(counts[...], scored, preferred_element_type=F32)
    ctx_ref[...] = silu(summed + bias_ref[...].astype(F32)).astype(BF16)

    for copy in exchange:
        copy.wait_send()
    swap.wait_send()

    @pl.when(is_even)
    def _():
        drain(reqout.at[pl.ds(0, PEERS - 1)], req_s)
        drain(repout.at[pl.ds(0, PEERS - 1)], rep_s)

    @pl.when(p == 1)
    def _():
        drain(reqout, req_s)
        drain(repout, rep_s)

    drain(xcols.at[pl.ds(0, MP - 1)], ag_s.at[0])
    drain(nrm.at[1, pl.ds(0, MP - 1)], ag_s.at[1])
    drain(states.at[pl.ds(0, MP - 1)], ag_s.at[2])
    for sec in range(2):
        drain(part.at[sec, pl.ds(0, MP - 1)], rs_s.at[sec])
    write.wait()


def on_device(
    item_owner, item_row, segments, neighbors, table, gains, w_in, w_out, w_ctx, ctx_bias
):
    n_rows = item_row.shape[0]
    vmem = pl.BlockSpec(memory_space=pltpu.VMEM)
    hbm = pl.BlockSpec(memory_space=pl.ANY)
    dma = pltpu.SemaphoreType.DMA
    states, ctx = pl.pallas_call(
        kernel,
        out_shape=(
            jax.ShapeDtypeStruct((MP, OWN, D), BF16),
            jax.ShapeDtypeStruct((ROWS, HD), BF16),
        ),
        in_specs=[vmem] * 6 + [hbm] * 4,
        out_specs=(hbm, vmem),
        scratch_shapes=[
            pltpu.VMEM((D, HD), BF16),
            pltpu.VMEM((2, 4 * D, HD), BF16),
            pltpu.VMEM((2, D, 4 * HD), BF16),
            pltpu.VMEM((2, HD, D), BF16),
            pltpu.VMEM((D, HD), BF16),
            pltpu.VMEM((2, 8, D), F32),
            pltpu.VMEM((PEERS, 1, HD), I32),
            pltpu.VMEM((PEERS, 1, HD), I32),
            pltpu.VMEM((PEERS, SLOTS, HD), BF16),
            pltpu.VMEM((PEERS, SLOTS, HD), BF16),
            pltpu.VMEM((2, ROWS, PEERS * SLOTS), BF16),
            pltpu.VMEM((2, ROWS, HD), BF16),
            pltpu.VMEM((ROWS, HD), BF16),
            pltpu.VMEM((MP, ROWS, HD), BF16),
            pltpu.VMEM((ROWS, ROWS), F32),
            pltpu.VMEM((ROWS, ROWS), BF16),
            pltpu.VMEM((2, MP, OWN, D), BF16),
            pltpu.VMEM((2, MP, OWN, D), BF16),
            pltpu.VMEM((2, MP, OWN, D), BF16),
            pltpu.VMEM((OWN, D), F32),
            pltpu.VMEM((MP, OWN, D), BF16),
            dma((4,)),
            dma(()),
            dma(()),
            dma(()),
            dma(()),
            dma((3,)),
            dma((3,)),
            dma(()),
            dma(()),
            dma((3,)),
            dma((3,)),
            dma((2,)),
            dma((2, MP)),
            dma(()),
        ],
        compiler_params=pltpu.CompilerParams(
            collective_id=0, has_side_effects=True, vmem_limit_bytes=60 * 1024 * 1024
        ),
        name="cascade",
    )(
        item_owner.reshape(1, n_rows),
        item_row.reshape(1, n_rows),
        segments[0],
        jnp.swapaxes(neighbors[0], 1, 2),
        gains,
        ctx_bias.reshape(1, -1),
        table,
        w_in.reshape(4 * D, HD),
        w_out[0],
        w_ctx,
    )
    return states.reshape(1, 1, ROWS, D), ctx.reshape(1, 1, ROWS, HD)


def solution(mesh):
    in_specs = (
        P("dp", None),
        P("dp"),
        P("dp", None, None),
        P("dp", None, None, None),
        P("dp", None),
        P("phase", None),
        P("phase", None, None, "mp"),
        P("phase", "mp", None),
        P(None, "mp"),
        P("mp"),
    )
    out_specs = (P("dp", "phase", None, None), P("dp", "phase", None, "mp"))
    return jax.shard_map(
        on_device, mesh=mesh, in_specs=in_specs, out_specs=out_specs, check_vma=False
    )
```

```python
import functools

import jax
import jax.numpy as jnp
from jax import lax
from jax.experimental import pallas as pl
from jax.experimental.pallas import tpu as pltpu
from jax.sharding import PartitionSpec as P

MESH = pl.DeviceIdType.MESH
F32 = jnp.float32
BF16 = jnp.bfloat16
I32 = jnp.int32

D = 1024
HD = 128
NBR = 8
ROWS = 256
MP = 8
ZN = 12
YN = 4
PEERS = ZN // 2 * YN
SLOTS = 32
OWN = ROWS // MP
EPS = 1e-06


def silu(x):
    half = 0.5 * x
    return half * (1.0 + jnp.tanh(half))


def iota(shape, axis):
    return lax.broadcasted_iota(I32, shape, axis)


def to_column(row):
    n = row.shape[1]
    diag = iota((n, n), 0) == iota((n, n), 1)
    return jnp.sum(jnp.where(diag, jnp.broadcast_to(row, (n, n)), 0.0), axis=1, keepdims=True)


def kernel(
    owner_ref, item_ref, seg_ref, nbr_ref, gain_ref, bias_ref, table_hbm, w_hbm, wo_hbm, wctx_hbm,
    out_hbm, ctx_ref,
    tcol, w4, wp, wo, wctx, gbuf, reqout, reqin, repout, repin, pick, part0, partin, xown, xcols,
    mask, counts, nrm, part, pairin, pairsum, rsin, xrow, last, states,
    loc, req_s, req_r, rep_s, rep_r, wex_s, wex_r, gex_s, gex_r, xp_s, xp_r, ag_s, ag0_r, ag1_r,
    pair_s, pair_r, rs_s, rs_r, fin_s, fin_r, out_s,
):
    g = lax.axis_index("dp")
    m = lax.axis_index("mp")
    p = lax.axis_index("phase")
    q = 1 - p
    zg, yg = g // YN, g % YN
    slot_me = (zg // 2) * YN + yg
    is_even = p == 0
    y, x = m // 4, m % 4
    batch = x // 2
    i = x % 2
    chip = 2 * y + i
    m_x = m + 1 - 2 * i
    m_y = lax.rem(m + 4, MP)
    m_d = lax.rem(m_x + 4, MP)
    near_m = (m_x, m_y, m_d)
    near_chip = (2 * y + 1 - i, 2 * (1 - y) + i, 2 * (1 - y) + 1 - i)
    twin = 4 * y + 3 - x
    block = 4 * p + chip
    at_home = p == batch
    away = p != batch
    sibling = (g, m, q)

    def dp_peer(j, dy):
        z = lax.rem(zg + 2 * j + p, ZN)
        yy = lax.rem(yg + dy, YN)
        o = z * YN + yy
        return (o, m_y if dy == 2 else m, p), (z // 2) * YN + yy

    def remote(src, dst, s, r, dev):
        return pltpu.make_async_remote_copy(
            src_ref=src, dst_ref=dst, send_sem=s, recv_sem=r, device_id=dev, device_id_type=MESH
        )

    def drain(ref, sem):
        pltpu.make_async_copy(ref, ref, sem).wait()

    barrier = pltpu.get_barrier_semaphore()

    def greet(dev):
        pl.semaphore_signal(barrier, inc=1, device_id=dev, device_id_type=MESH)

    far_first = (3, 2, 4, 1, 5, 0)
    dy_order = (2, 1, 3, 0)
    for j in far_first:
        for dy in dy_order:
            dev, _ = dp_peer(j, dy)
            if (j, dy) == (0, 0):
                @pl.when(p == 1)
                def _():
                    greet(dev)
            else:
                greet(dev)
    for d in range(1, MP):
        for core in range(2):
            greet((g, lax.rem(m + d, MP), core))
    greet(sibling)

    loads = []
    for n, column in enumerate((m, m_y)):
        col0 = pl.multiple_of(column * HD, HD)
        loads.append(
            pltpu.make_async_copy(
                table_hbm.at[:, pl.ds(col0, HD)], tcol.at[:, n * HD : (n + 1) * HD], loc.at[n]
            )
        )
    loads.append(pltpu.make_async_copy(wctx_hbm, wctx, loc.at[2]))
    for load in loads:
        load.start()

    @pl.when(is_even)
    def _():
        pltpu.make_async_copy(w_hbm, w4.at[0], wex_r.at[0, 0]).start()
        pltpu.make_async_copy(wo_hbm, wo.at[0], wex_r.at[1, 0]).start()

    gbuf[p] = jnp.broadcast_to(gain_ref[...].astype(F32), (8, D))

    n_rows = owner_ref.shape[1]
    owners = owner_ref[...]
    items = item_ref[...]
    slot_col = iota((PEERS, n_rows), 0)
    owner_of_slot = (2 * (slot_col // YN) + lax.rem(zg + p, 2)) * YN + slot_col % YN
    hit = (jnp.broadcast_to(owners, (PEERS, n_rows)) == owner_of_slot).astype(F32)
    before = (iota((n_rows, n_rows), 0) < iota((n_rows, n_rows), 1)).astype(F32).astype(BF16)
    count = jnp.dot(hit.astype(BF16), before, preferred_element_type=F32)
    rank = jnp.sum(hit * count, axis=0, keepdims=True)
    mine = jnp.sum(hit, axis=0, keepdims=True)
    slot_row = jnp.sum(hit * slot_col.astype(F32), axis=0, keepdims=True)
    key = jnp.where(mine > 0.5, slot_row * SLOTS + rank, -1.0)
    ranked = jnp.where(mine > 0.5, rank, -1.0)
    at_rank = (iota((HD, n_rows), 0).astype(F32) == jnp.broadcast_to(ranked, (HD, n_rows)))
    at_rank = at_rank.astype(F32).astype(BF16)
    hi = (items >> 5).astype(F32)
    lo = (items & 31).astype(F32)
    both = jnp.concatenate([hit * hi, hit * lo], axis=0).astype(BF16)
    found = lax.dot_general(both, at_rank, (((1,), (1,)), ((), ())), preferred_element_type=F32)
    wanted = (found[:PEERS] * 32.0 + found[PEERS:]).astype(I32)
    for s in range(PEERS):
        reqout[s] = wanted[s : s + 1]

    pl.semaphore_wait(barrier, 38 + p)

    def to_peers(src_of, dst, s_sem, r_sem, js):
        for j in js:
            for dy in dy_order:
                dev, s = dp_peer(j, dy)
                if (j, dy) == (0, 0):
                    @pl.when(is_even)
                    def _():
                        pltpu.make_async_copy(src_of.at[s], dst.at[slot_me], r_sem).start()

                    @pl.when(p == 1)
                    def _():
                        remote(src_of.at[s], dst.at[slot_me], s_sem, r_sem, dev).start()
                else:
                    remote(src_of.at[s], dst.at[slot_me], s_sem, r_sem, dev).start()

    to_peers(reqout, reqin, req_s, req_r, far_first)

    def send_weights(sec, dev):
        remote(w_hbm, w4.at[sec], wex_s.at[0], wex_r.at[0, sec], dev).start()
        remote(wo_hbm, wo.at[sec], wex_s.at[1], wex_r.at[1, sec], dev).start()

    gains = remote(gbuf.at[p], gbuf.at[p], gex_s, gex_r, sibling)
    gains.start()

    @pl.when(is_even)
    def _():
        send_weights(0, (g, twin, 1))

    @pl.when(p == 1)
    def _():
        send_weights(1, (g, m, 0))

    per_chunk = 64
    src_col = iota((4 * per_chunk, 4 * per_chunk), 1)
    dst_row = iota((4 * per_chunk, 4 * per_chunk), 0)
    spread = (src_col == 4 * (dst_row % per_chunk) + dst_row // per_chunk).astype(F32).astype(BF16)

    def arrange(sec):
        drain(w4.at[sec], wex_r.at[0, sec])
        drain(wo.at[sec], wex_r.at[1, sec])

        def body(n, carry):
            base = pl.multiple_of(n * 4 * per_chunk, 4 * per_chunk)
            moved = jnp.dot(spread, w4[sec, pl.ds(base, 4 * per_chunk), :], preferred_element_type=F32)
            moved = moved.astype(BF16)
            to = pl.multiple_of(n * per_chunk, per_chunk)
            for c in range(4):
                wp[sec, pl.ds(to, per_chunk), c * HD : (c + 1) * HD] = moved[
                    c * per_chunk : (c + 1) * per_chunk
                ]
            return carry

        lax.fori_loop(0, D // per_chunk, body, 0)

    key_col = to_column(key)
    for h in range(2):
        lanes = iota((ROWS, PEERS * SLOTS), 1).astype(F32)
        pick[h] = (key_col[h * ROWS : (h + 1) * ROWS] == lanes).astype(F32).astype(BF16)

    loads[0].wait()
    loads[1].wait()
    drain(reqin, req_r)
    crossed = lax.rem(yg + 2, YN)
    for pair in ((3, 2), (4, 1), (5, 0)):
        columns = []
        for j in pair:
            base = (lax.rem(zg + 2 * j + p, ZN) // 2) * YN
            asked = jnp.broadcast_to(reqin[pl.ds(base, YN)], (YN, SLOTS, HD))
            on = iota((YN, SLOTS, HD), 1) == iota((YN, SLOTS, HD), 2)
            columns.append(
                jnp.sum(jnp.where(on, asked.astype(F32), 0.0), axis=2, keepdims=True).reshape(
                    YN * SLOTS, 1
                )
            )
        column = jnp.concatenate(columns, axis=0)
        size = 2 * YN * SLOTS
        hot = (column == iota((size, D), 1).astype(F32)).astype(F32).astype(BF16)
        rows = jnp.dot(hot, tcol[...], preferred_element_type=F32)
        group = (iota((size, HD), 0) // SLOTS) % YN
        rows = jnp.where(group == crossed, rows[:, HD:], rows[:, :HD]).astype(BF16)
        rows = rows.reshape(2, YN, SLOTS, HD)
        for n, j in enumerate(pair):
            base = (lax.rem(zg + 2 * j + p, ZN) // 2) * YN
            repout[pl.ds(base, YN)] = rows[n]
        to_peers(repout, repin, rep_s, rep_r, pair)

    @pl.when(p == 1)
    def _():
        send_weights(1, (g, twin, 1))

    seg = seg_ref[pl.ds(batch, 1), :].astype(F32)
    seg_col = to_column(seg)
    below = iota((ROWS, ROWS), 1) <= iota((ROWS, ROWS), 0)
    same = seg_col == jnp.broadcast_to(seg, (ROWS, ROWS))
    mask[...] = jnp.where(below & same, 1.0 / ROWS, 0.0)
    hits = jnp.zeros((ROWS, ROWS), F32)
    near = nbr_ref[p]
    for n in range(NBR):
        row = jnp.broadcast_to(near[n : n + 1], (ROWS, ROWS))
        hits = hits + jnp.where(row == iota((ROWS, ROWS), 0), 1.0 / NBR, 0.0)
    counts[...] = hits.T.astype(BF16)
    arrange(0)
    gains.wait_recv()

    drain(repin, rep_r)
    for h in range(2):
        part0[h] = jnp.dot(
            pick[h], repin[...].reshape(PEERS * SLOTS, HD), preferred_element_type=F32
        ).astype(BF16)
    swap = remote(part0.at[q], partin, xp_s, xp_r, sibling)
    swap.start()
    swap.wait_recv()
    own = part0[p] + partin[...]
    xown[...] = own

    @pl.when(at_home)
    def _():
        for to in (m_d, m_y, m_x):
            remote(xown, xcols.at[m], ag_s.at[0], ag0_r.at[m], (g, to, y)).start()
        remote(xown, xcols.at[m], ag_s.at[0], ag0_r.at[m], sibling).start()
        xcols[m] = own

    @pl.when(away)
    def _():
        for row in (1 - y, y):
            for n in range(2):
                to = 4 * row + 2 * p + n
                remote(xown, xcols.at[m], ag_s.at[0], ag0_r.at[m], (g, to, y)).start()

    def pass_on(src):
        drain(xcols.at[src], ag0_r.at[src])
        remote(xcols.at[src], xcols.at[src], ag_s.at[0], ag0_r.at[src], sibling).start()

    for d in (1, 3, 2):
        pass_on(4 * p + lax.rem(x + d, 4))

    @pl.when(y != p)
    def _():
        pass_on(4 * p + x)

    @pl.when((y != p) & away)
    def _():
        drain(xcols.at[m], ag0_r.at[m])

    @pl.when(y == p)
    def _():
        drain(xcols.at[m_y], ag0_r.at[m_y])

    @pl.when((y == p) & away)
    def _():
        drain(xcols.at[m], ag0_r.at[m])

    for d in (1, 3, 2):
        src = 4 * q + lax.rem(x + d, 4)
        drain(xcols.at[src], ag0_r.at[src])

    total = jnp.zeros((ROWS, 1), F32)
    for c in range(MP):
        piece = xcols[c].astype(F32)
        total = total + jnp.sum(piece * piece, axis=1, keepdims=True)
    inv = lax.rsqrt(total * (1.0 / D) + EPS)
    for c in range(MP):
        scaled = xcols[c].astype(F32) * inv * gbuf[0, 0:1, c * HD : (c + 1) * HD]
        nrm[0, :, :, c * HD : (c + 1) * HD] = scaled.astype(BF16).reshape(MP, OWN, HD)
    own_row = pl.multiple_of(block * OWN, OWN)
    for c in range(MP):
        xrow[:, c * HD : (c + 1) * HD] = xcols[c, pl.ds(own_row, OWN), :].astype(F32)

    for sec in range(2):
        proj = jnp.dot(
            nrm[sec].reshape(ROWS, D), wp[sec], preferred_element_type=F32
        )
        proj = silu(proj).astype(BF16)
        gate, value = proj[:, :HD], proj[:, HD : 2 * HD]
        query, keys = proj[:, 2 * HD : 3 * HD], proj[:, 3 * HD :]
        scores = lax.dot_general(
            query, keys, (((1,), (1,)), ((), ())), preferred_element_type=F32
        ) * HD ** (-0.5)
        attn = (silu(scores) * mask[...]).astype(BF16)
        mixed = jnp.dot(attn, value, preferred_element_type=F32)
        mixed = mixed * lax.rsqrt(jnp.mean(mixed * mixed, axis=1, keepdims=True) + EPS)
        gated = (mixed * gate.astype(F32)).astype(BF16)
        back = jnp.dot(gated, wo[sec], preferred_element_type=F32).astype(BF16)
        part[sec] = back.reshape(MP, OWN, D)
        order = (near_chip[2], near_chip[1], near_chip[0], chip)
        for c in order:
            remote(
                part.at[sec, 4 * q + c], pairin.at[sec, c], pair_s.at[sec], pair_r.at[sec, c], sibling
            ).start()
        for n in (2, 1, 0):
            c = near_chip[n]
            drain(pairin.at[sec, c], pair_r.at[sec, c])
            pairsum[sec, n] = part[sec, 4 * p + c] + pairin[sec, c]
            remote(
                pairsum.at[sec, n], rsin.at[sec, n], rs_s.at[sec], rs_r.at[sec, n],
                (g, near_m[n], p),
            ).start()
        drain(pairin.at[sec, chip], pair_r.at[sec, chip])
        acc = part[sec, block].astype(F32) + pairin[sec, chip].astype(F32)
        if sec == 0:
            arrange(1)
        for n in (0, 1, 2):
            drain(rsin.at[sec, n], rs_r.at[sec, n])
            acc = acc + rsin[sec, n].astype(F32)
        new = (xrow[...] + acc).astype(BF16)
        if sec == 0:
            newf = new.astype(F32)
            xrow[...] = newf
            inv = lax.rsqrt(jnp.mean(newf * newf, axis=1, keepdims=True) + EPS)
            nrm[1, block] = (newf * inv * gbuf[1, 0:1, :]).astype(BF16)
            mine_now = nrm.at[1, block]
            for n in (2, 1, 0):
                remote(mine_now, mine_now, ag_s.at[1], ag1_r.at[block], (g, near_m[n], p)).start()
            remote(mine_now, mine_now, ag_s.at[1], ag1_r.at[block], sibling).start()
            for n in (0, 1, 2):
                e = 4 * p + near_chip[n]
                got = nrm.at[1, e]
                drain(got, ag1_r.at[e])
                remote(got, got, ag_s.at[1], ag1_r.at[e], sibling).start()
            for c in (chip,) + near_chip:
                drain(nrm.at[1, 4 * q + c], ag1_r.at[4 * q + c])
        else:
            last[...] = new
            for d in (4, 2, 6, 5, 7, 1, 3):
                to = lax.rem(m + d, MP)
                remote(last, states.at[block], fin_s, fin_r, (g, to, batch)).start()

            @pl.when(at_home)
            def _():
                states[block] = new
                drain(states.at[pl.ds(0, MP - 1)], fin_r)

            @pl.when(away)
            def _():
                remote(last, states.at[block], fin_s, fin_r, sibling).start()
                drain(states, fin_r)

    write = pltpu.make_async_copy(states, out_hbm, out_s)
    write.start()
    loads[2].wait()
    scored = jnp.dot(
        states[...].reshape(ROWS, D), wctx[...], preferred_element_type=F32
    ).astype(BF16)
    summed = jnp.dot(counts[...], scored, preferred_element_type=F32)
    ctx_ref[...] = silu(summed + bias_ref[...].astype(F32)).astype(BF16)

    gains.wait_send()
    swap.wait_send()
    drain(w4.at[0], wex_s.at[0])
    drain(wo.at[0], wex_s.at[1])
    drain(nrm.at[1, pl.ds(0, MP - 1)], ag_s.at[1])
    drain(xcols.at[pl.ds(0, MP - 1)], ag_s.at[0])
    drain(states.at[pl.ds(0, MP - 1)], fin_s)
    for sec in range(2):
        drain(pairin.at[sec], pair_s.at[sec])
        drain(pairsum.at[sec], rs_s.at[sec])

    @pl.when(y != p)
    def _():
        drain(xcols.at[0], ag_s.at[0])

    @pl.when(away)
    def _():
        drain(states.at[0], fin_s)

    @pl.when(is_even)
    def _():
        drain(reqout.at[pl.ds(0, PEERS - 1)], req_s)
        drain(repout.at[pl.ds(0, PEERS - 1)], rep_s)

    @pl.when(p == 1)
    def _():
        drain(reqout, req_s)
        drain(repout, rep_s)
        drain(w4.at[0], wex_s.at[0])
        drain(wo.at[0], wex_s.at[1])

    write.wait()


def on_device(
    item_owner, item_row, segments, neighbors, table, gains, w_in, w_out, w_ctx, ctx_bias
):
    n_rows = item_row.shape[0]
    vmem = pl.BlockSpec(memory_space=pltpu.VMEM)
    hbm = pl.BlockSpec(memory_space=pl.ANY)
    dma = pltpu.SemaphoreType.DMA
    states, ctx = pl.pallas_call(
        kernel,
        out_shape=(
            jax.ShapeDtypeStruct((MP, OWN, D), BF16),
            jax.ShapeDtypeStruct((ROWS, HD), BF16),
        ),
        in_specs=[vmem] * 6 + [hbm] * 4,
        out_specs=(hbm, vmem),
        scratch_shapes=[
            pltpu.VMEM((D, 2 * HD), BF16),
            pltpu.VMEM((2, 4 * D, HD), BF16),
            pltpu.VMEM((2, D, 4 * HD), BF16),
            pltpu.VMEM((2, HD, D), BF16),
            pltpu.VMEM((D, HD), BF16),
            pltpu.VMEM((2, 8, D), F32),
            pltpu.VMEM((PEERS, 1, HD), I32),
            pltpu.VMEM((PEERS, 1, HD), I32),
            pltpu.VMEM((PEERS, SLOTS, HD), BF16),
            pltpu.VMEM((PEERS, SLOTS, HD), BF16),
            pltpu.VMEM((2, ROWS, PEERS * SLOTS), BF16),
            pltpu.VMEM((2, ROWS, HD), BF16),
            pltpu.VMEM((ROWS, HD), BF16),
            pltpu.VMEM((ROWS, HD), BF16),
            pltpu.VMEM((MP, ROWS, HD), BF16),
            pltpu.VMEM((ROWS, ROWS), F32),
            pltpu.VMEM((ROWS, ROWS), BF16),
            pltpu.VMEM((2, MP, OWN, D), BF16),
            pltpu.VMEM((2, MP, OWN, D), BF16),
            pltpu.VMEM((2, 4, OWN, D), BF16),
            pltpu.VMEM((2, 3, OWN, D), BF16),
            pltpu.VMEM((2, 3, OWN, D), BF16),
            pltpu.VMEM((OWN, D), F32),
            pltpu.VMEM((OWN, D), BF16),
            pltpu.VMEM((MP, OWN, D), BF16),
            dma((3,)),
            dma(()),
            dma(()),
            dma(()),
            dma(()),
            dma((2,)),
            dma((2, 2)),
            dma(()),
            dma(()),
            dma(()),
            dma(()),
            dma((2,)),
            dma((MP,)),
            dma((MP,)),
            dma((2,)),
            dma((2, 4)),
            dma((2,)),
            dma((2, 3)),
            dma(()),
            dma(()),
            dma(()),
        ],
        compiler_params=pltpu.CompilerParams(
            collective_id=0, has_side_effects=True, vmem_limit_bytes=60 * 1024 * 1024
        ),
        name="cascade",
    )(
        item_owner.reshape(1, n_rows),
        item_row.reshape(1, n_rows),
        segments[0],
        jnp.swapaxes(neighbors[0], 1, 2),
        gains,
        ctx_bias.reshape(1, -1),
        table,
        w_in.reshape(4 * D, HD),
        w_out[0],
        w_ctx,
    )
    return states.reshape(1, 1, ROWS, D), ctx.reshape(1, 1, ROWS, HD)


def solution(mesh):
    in_specs = (
        P("dp", None),
        P("dp"),
        P("dp", None, None),
        P("dp", None, None, None),
        P("dp", None),
        P("phase", None),
        P("phase", None, None, "mp"),
        P("phase", "mp", None),
        P(None, "mp"),
        P("mp"),
    )
    out_specs = (P("dp", "phase", None, None), P("dp", "phase", None, "mp"))
    return jax.shard_map(
        on_device, mesh=mesh, in_specs=in_specs, out_specs=out_specs, check_vma=False
    )
```

```python
import functools

import jax
import jax.numpy as jnp
from jax import lax
from jax.experimental import pallas as pl
from jax.experimental.pallas import tpu as pltpu
from jax.sharding import PartitionSpec as P

MESH = pl.DeviceIdType.MESH
F32 = jnp.float32
BF16 = jnp.bfloat16
I32 = jnp.int32

D = 1024
HD = 128
NBR = 8
ROWS = 256
MP = 8
ZN = 12
YN = 4
PEERS = ZN // 2 * YN
SLOTS = 32
HALF = ROWS // 2
OWN = HALF // MP
EPS = 1e-06


def silu(x):
    half = 0.5 * x
    return half * (1.0 + jnp.tanh(half))


def iota(shape, axis):
    return lax.broadcasted_iota(I32, shape, axis)


def to_column(row):
    n = row.shape[1]
    diag = iota((n, n), 0) == iota((n, n), 1)
    return jnp.sum(jnp.where(diag, jnp.broadcast_to(row, (n, n)), 0.0), axis=1, keepdims=True)


def kernel(
    owner_ref, item_ref, seg_ref, nbr_ref, gain_ref, bias_ref, table_hbm, w_hbm, wo_hbm, wctx_hbm,
    out_hbm, ctx_ref,
    tcol, w4, wp, wo, wctx, gbuf, reqout, reqin, repout, repin, pick, part0, partin, xcols,
    mask, counts, nrm, feats, part, rsin, xrow, states,
    loc, req_s, req_r, rep_s, rep_r, wex_s, wex_r, xp_s, xp_r, ag_s, ag_r, rs_s, rs_r, out_s,
):
    g = lax.axis_index("dp")
    m = lax.axis_index("mp")
    p = lax.axis_index("phase")
    q = 1 - p
    zg, yg = g // YN, g % YN
    slot_me = (zg // 2) * YN + yg
    is_even = p == 0

    def dp_peer(j, dy):
        z = lax.rem(zg + 2 * j + p, ZN)
        y = lax.rem(yg + dy, YN)
        return z * YN + y, (z // 2) * YN + y

    def mp_peer(d):
        return lax.rem(m + d, MP)

    def remote(src, dst, s, r, dev):
        return pltpu.make_async_remote_copy(
            src_ref=src, dst_ref=dst, send_sem=s, recv_sem=r, device_id=dev, device_id_type=MESH
        )

    def drain(ref, sem):
        pltpu.make_async_copy(ref, ref, sem).wait()

    barrier = pltpu.get_barrier_semaphore()

    def greet(dev):
        pl.semaphore_signal(barrier, inc=1, device_id=dev, device_id_type=MESH)

    far_first = (3, 2, 4, 1, 5, 0)
    for j in far_first:
        for dy in (2, 1, 3, 0):
            o, _ = dp_peer(j, dy)
            if (j, dy) == (0, 0):
                @pl.when(p == 1)
                def _():
                    greet((o, m, p))
            else:
                greet((o, m, p))
    for d in range(1, MP):
        greet((g, mp_peer(d), p))
    greet((g, m, q))

    col0 = pl.multiple_of(m * HD, HD)
    loads = [
        pltpu.make_async_copy(table_hbm.at[:, pl.ds(col0, HD)], tcol, loc.at[0]),
        pltpu.make_async_copy(w_hbm, w4.at[p], loc.at[1]),
        pltpu.make_async_copy(wo_hbm, wo.at[p], loc.at[2]),
        pltpu.make_async_copy(wctx_hbm, wctx, loc.at[3]),
    ]
    for load in loads:
        load.start()
    gbuf[p] = jnp.broadcast_to(gain_ref[...].astype(F32), (8, D))

    n_rows = owner_ref.shape[1]
    owners = owner_ref[...]
    items = item_ref[...]
    slot_col = iota((PEERS, n_rows), 0)
    owner_of_slot = (2 * (slot_col // YN) + lax.rem(zg + p, 2)) * YN + slot_col % YN
    hit = (jnp.broadcast_to(owners, (PEERS, n_rows)) == owner_of_slot).astype(F32)
    before = (iota((n_rows, n_rows), 0) < iota((n_rows, n_rows), 1)).astype(F32).astype(BF16)
    count = jnp.dot(hit.astype(BF16), before, preferred_element_type=F32)
    rank = jnp.sum(hit * count, axis=0, keepdims=True)
    mine = jnp.sum(hit, axis=0, keepdims=True)
    slot_row = jnp.sum(hit * slot_col.astype(F32), axis=0, keepdims=True)
    key = jnp.where(mine > 0.5, slot_row * SLOTS + rank, -1.0)
    ranked = jnp.where(mine > 0.5, rank, -1.0)
    at_rank = (iota((HD, n_rows), 0).astype(F32) == jnp.broadcast_to(ranked, (HD, n_rows)))
    at_rank = at_rank.astype(F32).astype(BF16)
    hi = (items >> 5).astype(F32)
    lo = (items & 31).astype(F32)
    both = jnp.concatenate([hit * hi, hit * lo], axis=0).astype(BF16)
    found = lax.dot_general(both, at_rank, (((1,), (1,)), ((), ())), preferred_element_type=F32)
    wanted = (found[:PEERS] * 32.0 + found[PEERS:]).astype(I32)
    for s in range(PEERS):
        reqout[s] = wanted[s : s + 1]

    pl.semaphore_wait(barrier, 31 + p)

    def to_peers(src_of, dst, s_sem, r_sem, js):
        for j in js:
            for dy in (2, 1, 3, 0):
                o, s = dp_peer(j, dy)
                if (j, dy) == (0, 0):
                    @pl.when(is_even)
                    def _():
                        pltpu.make_async_copy(src_of.at[s], dst.at[slot_me], r_sem).start()

                    @pl.when(p == 1)
                    def _():
                        remote(src_of.at[s], dst.at[slot_me], s_sem, r_sem, (o, m, p)).start()
                else:
                    remote(src_of.at[s], dst.at[slot_me], s_sem, r_sem, (o, m, p)).start()

    to_peers(reqout, reqin, req_s, req_r, far_first)

    loads[1].wait()
    loads[2].wait()
    sibling = (g, m, q)
    exchange = [
        remote(w4.at[p], w4.at[p], wex_s.at[0], wex_r.at[0], sibling),
        remote(wo.at[p], wo.at[p], wex_s.at[1], wex_r.at[1], sibling),
        remote(gbuf.at[p], gbuf.at[p], wex_s.at[2], wex_r.at[2], sibling),
    ]
    for copy in exchange:
        copy.start()

    per_chunk = 64
    src_col = iota((4 * per_chunk, 4 * per_chunk), 1)
    dst_row = iota((4 * per_chunk, 4 * per_chunk), 0)
    spread = (src_col == 4 * (dst_row % per_chunk) + dst_row // per_chunk).astype(F32).astype(BF16)

    def arrange(sec):
        def body(i, carry):
            base = pl.multiple_of(i * 4 * per_chunk, 4 * per_chunk)
            moved = jnp.dot(spread, w4[sec, pl.ds(base, 4 * per_chunk), :], preferred_element_type=F32)
            moved = moved.astype(BF16)
            to = pl.multiple_of(i * per_chunk, per_chunk)
            for c in range(4):
                wp[sec, pl.ds(to, per_chunk), c * HD : (c + 1) * HD] = moved[
                    c * per_chunk : (c + 1) * per_chunk
                ]
            return carry

        lax.fori_loop(0, D // per_chunk, body, 0, unroll=True)

    arrange(p)
    key_col = to_column(key)
    for h in range(2):
        lanes = iota((ROWS, PEERS * SLOTS), 1).astype(F32)
        pick[h] = (key_col[h * ROWS : (h + 1) * ROWS] == lanes).astype(F32).astype(BF16)

    loads[0].wait()
    drain(reqin, req_r)
    for pair in ((3, 2), (4, 1), (5, 0)):
        columns = []
        for j in pair:
            z = lax.rem(zg + 2 * j + p, ZN)
            base = (z // 2) * YN
            asked = jnp.broadcast_to(reqin[pl.ds(base, YN)], (YN, SLOTS, HD))
            on = iota((YN, SLOTS, HD), 1) == iota((YN, SLOTS, HD), 2)
            columns.append(
                jnp.sum(jnp.where(on, asked.astype(F32), 0.0), axis=2, keepdims=True).reshape(
                    YN * SLOTS, 1
                )
            )
        column = jnp.concatenate(columns, axis=0)
        size = 2 * YN * SLOTS
        hot = (column == iota((size, D), 1).astype(F32)).astype(F32).astype(BF16)
        rows = jnp.dot(hot, tcol[...], preferred_element_type=F32).astype(BF16)
        rows = rows.reshape(2, YN, SLOTS, HD)
        for i, j in enumerate(pair):
            z = lax.rem(zg + 2 * j + p, ZN)
            repout[pl.ds((z // 2) * YN, YN)] = rows[i]
        to_peers(repout, repin, rep_s, rep_r, pair)

    exchange[0].wait_recv()
    exchange[1].wait_recv()
    exchange[2].wait_recv()
    arrange(q)
    seg = seg_ref[pl.ds(p, 1), :].astype(F32)
    seg_col = to_column(seg)
    below = iota((ROWS, ROWS), 1) <= iota((ROWS, ROWS), 0)
    same = seg_col == jnp.broadcast_to(seg, (ROWS, ROWS))
    mask[...] = jnp.where(below & same, 1.0 / ROWS, 0.0)
    hits = jnp.zeros((ROWS, ROWS), F32)
    near = nbr_ref[p]
    for n in range(NBR):
        row = jnp.broadcast_to(near[n : n + 1], (ROWS, ROWS))
        hits = hits + jnp.where(row == iota((ROWS, ROWS), 0), 1.0 / NBR, 0.0)
    counts[...] = hits.T.astype(BF16)

    drain(repin, rep_r)
    for h in range(2):
        part0[h] = jnp.dot(
            pick[h], repin[...].reshape(PEERS * SLOTS, HD), preferred_element_type=F32
        ).astype(BF16)
    swap = remote(part0.at[q], partin, xp_s, xp_r, sibling)
    swap.start()
    swap.wait_recv()
    own = part0[p] + partin[...]
    for h in range(2):
        xcols[h, m] = own[h * HALF : (h + 1) * HALF]

    def to_group(src_of, dst, s_sem, r_of):
        for d in (4, 2, 6, 5, 7, 1, 3):
            to = mp_peer(d)
            remote(src_of(to), dst, s_sem, r_of, (g, to, p)).start()

    for h in range(2):
        to_group(lambda to: xcols.at[h, m], xcols.at[h, m], ag_s.at[0], ag_r.at[0, h])

    own_row = pl.multiple_of(m * OWN, OWN)
    for sec in range(2):
        for h in range(2):
            if sec == 0:
                drain(xcols.at[h, pl.ds(0, MP - 1)], ag_r.at[0, h])
                total = jnp.zeros((HALF, 1), F32)
                for k in range(MP):
                    block = xcols[h, k].astype(F32)
                    total = total + jnp.sum(block * block, axis=1, keepdims=True)
                inv = lax.rsqrt(total * (1.0 / D) + EPS)
                for k in range(MP):
                    scaled = xcols[h, k].astype(F32) * inv * gbuf[0, 0:1, k * HD : (k + 1) * HD]
                    nrm[0, h, :, :, k * HD : (k + 1) * HD] = scaled.astype(BF16).reshape(MP, OWN, HD)
                    xrow[h, :, k * HD : (k + 1) * HD] = xcols[h, k, pl.ds(own_row, OWN), :].astype(F32)
            else:
                drain(nrm.at[1, h, pl.ds(0, MP - 1)], ag_r.at[1, h])
            proj = jnp.dot(nrm[sec, h].reshape(HALF, D), wp[sec], preferred_element_type=F32)
            proj = silu(proj).astype(BF16)
            rows = slice(h * HALF, (h + 1) * HALF)
            seen = slice(0, (h + 1) * HALF)
            feats[rows] = proj
            gate, query = proj[:, :HD], proj[:, 2 * HD : 3 * HD]
            scores = lax.dot_general(
                query, feats[seen, 3 * HD :], (((1,), (1,)), ((), ())), preferred_element_type=F32
            ) * HD ** (-0.5)
            attn = (silu(scores) * mask[rows, seen]).astype(BF16)
            mixed = jnp.dot(attn, feats[seen, HD : 2 * HD], preferred_element_type=F32)
            mixed = mixed * lax.rsqrt(jnp.mean(mixed * mixed, axis=1, keepdims=True) + EPS)
            gated = (mixed * gate.astype(F32)).astype(BF16)
            back = jnp.dot(gated, wo[sec], preferred_element_type=F32).astype(BF16)
            part[sec, h] = back.reshape(MP, OWN, D)
            to_group(
                lambda to: part.at[sec, h, to], rsin.at[sec, h, m], rs_s.at[sec], rs_r.at[sec, h, m]
            )
        for h in range(2):
            acc = xrow[h] + part[sec, h, m].astype(F32)
            for d in (1, 3, 5, 7, 2, 6, 4):
                src = mp_peer(d)
                drain(rsin.at[sec, h, src], rs_r.at[sec, h, src])
                acc = acc + rsin[sec, h, src].astype(F32)
            new = acc.astype(BF16)
            if sec == 0:
                newf = new.astype(F32)
                xrow[h] = newf
                inv = lax.rsqrt(jnp.mean(newf * newf, axis=1, keepdims=True) + EPS)
                nrm[1, h, m] = (newf * inv * gbuf[1, 0:1, :]).astype(BF16)
                to_group(lambda to: nrm.at[1, h, m], nrm.at[1, h, m], ag_s.at[1], ag_r.at[1, h])
            else:
                states[h, m] = new
                to_group(lambda to: states.at[h, m], states.at[h, m], ag_s.at[2], ag_r.at[2, h])

    loads[3].wait()
    writes = []
    scored = []
    for h in range(2):
        drain(states.at[h, pl.ds(0, MP - 1)], ag_r.at[2, h])
        writes.append(pltpu.make_async_copy(states.at[h], out_hbm.at[h], out_s.at[h]))
        writes[h].start()
        scored.append(
            jnp.dot(
                states[h].reshape(HALF, D), wctx[...], preferred_element_type=F32
            ).astype(BF16)
        )
    summed = jnp.dot(
        counts[...], jnp.concatenate(scored, axis=0), preferred_element_type=F32
    )
    ctx_ref[...] = silu(summed + bias_ref[...].astype(F32)).astype(BF16)

    for copy in exchange:
        copy.wait_send()
    swap.wait_send()

    @pl.when(is_even)
    def _():
        drain(reqout.at[pl.ds(0, PEERS - 1)], req_s)
        drain(repout.at[pl.ds(0, PEERS - 1)], rep_s)

    @pl.when(p == 1)
    def _():
        drain(reqout, req_s)
        drain(repout, rep_s)

    for h in range(2):
        drain(xcols.at[h, pl.ds(0, MP - 1)], ag_s.at[0])
        drain(nrm.at[1, h, pl.ds(0, MP - 1)], ag_s.at[1])
        drain(states.at[h, pl.ds(0, MP - 1)], ag_s.at[2])
        for sec in range(2):
            drain(part.at[sec, h, pl.ds(0, MP - 1)], rs_s.at[sec])
        writes[h].wait()


def on_device(
    item_owner, item_row, segments, neighbors, table, gains, w_in, w_out, w_ctx, ctx_bias
):
    n_rows = item_row.shape[0]
    vmem = pl.BlockSpec(memory_space=pltpu.VMEM)
    hbm = pl.BlockSpec(memory_space=pl.ANY)
    dma = pltpu.SemaphoreType.DMA
    states, ctx = pl.pallas_call(
        kernel,
        out_shape=(
            jax.ShapeDtypeStruct((2, MP, OWN, D), BF16),
            jax.ShapeDtypeStruct((ROWS, HD), BF16),
        ),
        in_specs=[vmem] * 6 + [hbm] * 4,
        out_specs=(hbm, vmem),
        scratch_shapes=[
            pltpu.VMEM((D, HD), BF16),
            pltpu.VMEM((2, 4 * D, HD), BF16),
            pltpu.VMEM((2, D, 4 * HD), BF16),
            pltpu.VMEM((2, HD, D), BF16),
            pltpu.VMEM((D, HD), BF16),
            pltpu.VMEM((2, 8, D), F32),
            pltpu.VMEM((PEERS, 1, HD), I32),
            pltpu.VMEM((PEERS, 1, HD), I32),
            pltpu.VMEM((PEERS, SLOTS, HD), BF16),
            pltpu.VMEM((PEERS, SLOTS, HD), BF16),
            pltpu.VMEM((2, ROWS, PEERS * SLOTS), BF16),
            pltpu.VMEM((2, ROWS, HD), BF16),
            pltpu.VMEM((ROWS, HD), BF16),
            pltpu.VMEM((2, MP, HALF, HD), BF16),
            pltpu.VMEM((ROWS, ROWS), F32),
            pltpu.VMEM((ROWS, ROWS), BF16),
            pltpu.VMEM((2, 2, MP, OWN, D), BF16),
            pltpu.VMEM((ROWS, 4 * HD), BF16),
            pltpu.VMEM((2, 2, MP, OWN, D), BF16),
            pltpu.VMEM((2, 2, MP, OWN, D), BF16),
            pltpu.VMEM((2, OWN, D), F32),
            pltpu.VMEM((2, MP, OWN, D), BF16),
            dma((4,)),
            dma(()),
            dma(()),
            dma(()),
            dma(()),
            dma((3,)),
            dma((3,)),
            dma(()),
            dma(()),
            dma((3,)),
            dma((3, 2)),
            dma((2,)),
            dma((2, 2, MP)),
            dma((2,)),
        ],
        compiler_params=pltpu.CompilerParams(
            collective_id=0, has_side_effects=True, vmem_limit_bytes=60 * 1024 * 1024
        ),
        name="cascade",
    )(
        item_owner.reshape(1, n_rows),
        item_row.reshape(1, n_rows),
        segments[0],
        jnp.swapaxes(neighbors[0], 1, 2),
        gains,
        ctx_bias.reshape(1, -1),
        table,
        w_in.reshape(4 * D, HD),
        w_out[0],
        w_ctx,
    )
    return states.reshape(1, 1, ROWS, D), ctx.reshape(1, 1, ROWS, HD)


def solution(mesh):
    in_specs = (
        P("dp", None),
        P("dp"),
        P("dp", None, None),
        P("dp", None, None, None),
        P("dp", None),
        P("phase", None),
        P("phase", None, None, "mp"),
        P("phase", "mp", None),
        P(None, "mp"),
        P("mp"),
    )
    out_specs = (P("dp", "phase", None, None), P("dp", "phase", None, "mp"))
    return jax.shard_map(
        on_device, mesh=mesh, in_specs=in_specs, out_specs=out_specs, check_vma=False
    )
```

```python
import functools

import jax
import jax.numpy as jnp
from jax import lax
from jax.experimental import pallas as pl
from jax.experimental.pallas import tpu as pltpu
from jax.sharding import PartitionSpec as P

MESH = pl.DeviceIdType.MESH
F32 = jnp.float32
BF16 = jnp.bfloat16
I32 = jnp.int32

D = 1024
HD = 128
NBR = 8
ROWS = 256
MP = 8
ZN = 12
YN = 4
PEERS = ZN // 2 * YN
SLOTS = 24
HALF = ROWS // 2
OWN = HALF // MP
EPS = 1e-06


def silu(x):
    half = 0.5 * x
    return half * (1.0 + jnp.tanh(half))


def iota(shape, axis):
    return lax.broadcasted_iota(I32, shape, axis)


def to_column(row):
    n = row.shape[1]
    diag = iota((n, n), 0) == iota((n, n), 1)
    return jnp.sum(jnp.where(diag, jnp.broadcast_to(row, (n, n)), 0.0), axis=1, keepdims=True)


def kernel(
    owner_ref, item_ref, seg_ref, nbr_ref, gain_ref, table_hbm, w_hbm, wo_hbm, wctx_hbm,
    states, counts, wctx,
    tcol, w4, wp, wo, gbuf, reqout, reqin, repout, repin, pick, part0, partin, xcols,
    mask, nrm, feats, part, rsin, xrow,
    loc, req_s, req_r, rep_s, rep_r, wex_s, wex_r, xp_s, xp_r, ag_s, ag_r, rs_s, rs_r,
):
    g = lax.axis_index("dp")
    m = lax.axis_index("mp")
    p = lax.axis_index("phase")
    q = 1 - p
    zg, yg = g // YN, g % YN
    slot_me = (zg // 2) * YN + yg
    is_even = p == 0

    def dp_peer(j, dy):
        z = lax.rem(zg + 2 * j + p, ZN)
        y = lax.rem(yg + dy, YN)
        return z * YN + y, (z // 2) * YN + y

    def mp_peer(d):
        return lax.rem(m + d, MP)

    def remote(src, dst, s, r, dev):
        return pltpu.make_async_remote_copy(
            src_ref=src, dst_ref=dst, send_sem=s, recv_sem=r, device_id=dev, device_id_type=MESH
        )

    def drain(ref, sem):
        pltpu.make_async_copy(ref, ref, sem).wait()

    barrier = pltpu.get_barrier_semaphore()

    def greet(dev):
        pl.semaphore_signal(barrier, inc=1, device_id=dev, device_id_type=MESH)

    far_first = (3, 2, 4, 1, 5, 0)
    for j in far_first:
        for dy in (2, 1, 3, 0):
            o, _ = dp_peer(j, dy)
            if (j, dy) == (0, 0):
                @pl.when(p == 1)
                def _():
                    greet((o, m, p))
            else:
                greet((o, m, p))
    for d in range(1, MP):
        greet((g, mp_peer(d), p))
    greet((g, m, q))

    col0 = pl.multiple_of(m * HD, HD)
    loads = [
        pltpu.make_async_copy(table_hbm.at[:, pl.ds(col0, HD)], tcol, loc.at[0]),
        pltpu.make_async_copy(w_hbm, w4.at[p], loc.at[1]),
        pltpu.make_async_copy(wo_hbm, wo.at[p], loc.at[2]),
    ]
    keep = pltpu.make_async_copy(wctx_hbm, wctx, loc.at[3])
    keep.start()
    for load in loads:
        load.start()
    gbuf[p] = jnp.broadcast_to(gain_ref[...].astype(F32), (8, D))

    n_rows = owner_ref.shape[1]
    owners = owner_ref[...]
    items = item_ref[...]
    slot_col = iota((PEERS, n_rows), 0)
    owner_of_slot = (2 * (slot_col // YN) + lax.rem(zg + p, 2)) * YN + slot_col % YN
    hit = (jnp.broadcast_to(owners, (PEERS, n_rows)) == owner_of_slot).astype(F32)
    before = (iota((n_rows, n_rows), 0) < iota((n_rows, n_rows), 1)).astype(F32).astype(BF16)
    count = jnp.dot(hit.astype(BF16), before, preferred_element_type=F32)
    rank = jnp.sum(hit * count, axis=0, keepdims=True)
    mine = jnp.sum(hit, axis=0, keepdims=True)
    slot_row = jnp.sum(hit * slot_col.astype(F32), axis=0, keepdims=True)
    key = jnp.where(mine > 0.5, slot_row * SLOTS + rank, -1.0)
    ranked = jnp.where(mine > 0.5, rank, -1.0)
    at_rank = (iota((HD, n_rows), 0).astype(F32) == jnp.broadcast_to(ranked, (HD, n_rows)))
    at_rank = at_rank.astype(F32).astype(BF16)
    hi = (items >> 5).astype(F32)
    lo = (items & 31).astype(F32)
    both = jnp.concatenate([hit * hi, hit * lo], axis=0).astype(BF16)
    found = lax.dot_general(both, at_rank, (((1,), (1,)), ((), ())), preferred_element_type=F32)
    wanted = (found[:PEERS] * 32.0 + found[PEERS:]).astype(I32)
    for s in range(PEERS):
        reqout[s] = wanted[s : s + 1]

    pl.semaphore_wait(barrier, 31 + p)

    def to_peers(src_of, dst, s_sem, r_sem, js):
        for j in js:
            for dy in (2, 1, 3, 0):
                o, s = dp_peer(j, dy)
                if (j, dy) == (0, 0):
                    @pl.when(is_even)
                    def _():
                        pltpu.make_async_copy(src_of.at[s], dst.at[slot_me], r_sem).start()

                    @pl.when(p == 1)
                    def _():
                        remote(src_of.at[s], dst.at[slot_me], s_sem, r_sem, (o, m, p)).start()
                else:
                    remote(src_of.at[s], dst.at[slot_me], s_sem, r_sem, (o, m, p)).start()

    to_peers(reqout, reqin, req_s, req_r, far_first)

    loads[1].wait()
    loads[2].wait()
    sibling = (g, m, q)
    exchange = [
        remote(w4.at[p], w4.at[p], wex_s.at[0], wex_r.at[0], sibling),
        remote(wo.at[p], wo.at[p], wex_s.at[1], wex_r.at[1], sibling),
        remote(gbuf.at[p], gbuf.at[p], wex_s.at[2], wex_r.at[2], sibling),
    ]
    for copy in exchange:
        copy.start()

    per_chunk = 64
    src_col = iota((4 * per_chunk, 4 * per_chunk), 1)
    dst_row = iota((4 * per_chunk, 4 * per_chunk), 0)
    spread = (src_col == 4 * (dst_row % per_chunk) + dst_row // per_chunk).astype(F32).astype(BF16)

    def arrange(sec):
        def body(i, carry):
            base = pl.multiple_of(i * 4 * per_chunk, 4 * per_chunk)
            moved = jnp.dot(spread, w4[sec, pl.ds(base, 4 * per_chunk), :], preferred_element_type=F32)
            moved = moved.astype(BF16)
            to = pl.multiple_of(i * per_chunk, per_chunk)
            for c in range(4):
                wp[sec, pl.ds(to, per_chunk), c * HD : (c + 1) * HD] = moved[
                    c * per_chunk : (c + 1) * per_chunk
                ]
            return carry

        lax.fori_loop(0, D // per_chunk, body, 0, unroll=True)

    arrange(p)
    key_col = to_column(key)
    for h in range(2):
        lanes = iota((ROWS, PEERS * SLOTS), 1).astype(F32)
        pick[h] = (key_col[h * ROWS : (h + 1) * ROWS] == lanes).astype(F32).astype(BF16)

    loads[0].wait()
    drain(reqin, req_r)
    for pair in ((3, 2), (4, 1), (5, 0)):
        columns = []
        for j in pair:
            z = lax.rem(zg + 2 * j + p, ZN)
            base = (z // 2) * YN
            asked = jnp.broadcast_to(reqin[pl.ds(base, YN)], (YN, SLOTS, HD))
            on = iota((YN, SLOTS, HD), 1) == iota((YN, SLOTS, HD), 2)
            columns.append(
                jnp.sum(jnp.where(on, asked.astype(F32), 0.0), axis=2, keepdims=True).reshape(
                    YN * SLOTS, 1
                )
            )
        column = jnp.concatenate(columns, axis=0)
        size = 2 * YN * SLOTS
        hot = (column == iota((size, D), 1).astype(F32)).astype(F32).astype(BF16)
        rows = jnp.dot(hot, tcol[...], preferred_element_type=F32).astype(BF16)
        rows = rows.reshape(2, YN, SLOTS, HD)
        for i, j in enumerate(pair):
            z = lax.rem(zg + 2 * j + p, ZN)
            repout[pl.ds((z // 2) * YN, YN)] = rows[i]
        to_peers(repout, repin, rep_s, rep_r, pair)

    exchange[0].wait_recv()
    exchange[1].wait_recv()
    exchange[2].wait_recv()
    arrange(q)
    seg = seg_ref[pl.ds(p, 1), :].astype(F32)
    seg_col = to_column(seg)
    below = iota((ROWS, ROWS), 1) <= iota((ROWS, ROWS), 0)
    same = seg_col == jnp.broadcast_to(seg, (ROWS, ROWS))
    mask[...] = jnp.where(below & same, 1.0 / ROWS, 0.0)
    hits = jnp.zeros((ROWS, ROWS), F32)
    near = nbr_ref[p]
    for n in range(NBR):
        row = jnp.broadcast_to(near[n : n + 1], (ROWS, ROWS))
        hits = hits + jnp.where(row == iota((ROWS, ROWS), 0), 1.0 / NBR, 0.0)
    counts[...] = hits.T.astype(BF16)
    keep.wait()

    drain(repin, rep_r)
    for h in range(2):
        part0[h] = jnp.dot(
            pick[h], repin[...].reshape(PEERS * SLOTS, HD), preferred_element_type=F32
        ).astype(BF16)
    swap = remote(part0.at[q], partin, xp_s, xp_r, sibling)
    swap.start()
    swap.wait_recv()
    own = part0[p] + partin[...]
    for h in range(2):
        xcols[h, m] = own[h * HALF : (h + 1) * HALF]

    def to_group(src_of, dst, s_sem, r_of):
        for d in (4, 2, 6, 5, 7, 1, 3):
            to = mp_peer(d)
            remote(src_of(to), dst, s_sem, r_of, (g, to, p)).start()

    for h in range(2):
        to_group(lambda to: xcols.at[h, m], xcols.at[h, m], ag_s.at[0], ag_r.at[0, h])

    own_row = pl.multiple_of(m * OWN, OWN)
    for sec in range(2):
        for h in range(2):
            if sec == 0:
                drain(xcols.at[h, pl.ds(0, MP - 1)], ag_r.at[0, h])
                total = jnp.zeros((HALF, 1), F32)
                for k in range(MP):
                    block = xcols[h, k].astype(F32)
                    total = total + jnp.sum(block * block, axis=1, keepdims=True)
                inv = lax.rsqrt(total * (1.0 / D) + EPS)
                for k in range(MP):
                    scaled = xcols[h, k].astype(F32) * inv * gbuf[0, 0:1, k * HD : (k + 1) * HD]
                    nrm[0, h, :, :, k * HD : (k + 1) * HD] = scaled.astype(BF16).reshape(MP, OWN, HD)
                    xrow[h, :, k * HD : (k + 1) * HD] = xcols[h, k, pl.ds(own_row, OWN), :].astype(F32)
            else:
                drain(nrm.at[1, h, pl.ds(0, MP - 1)], ag_r.at[1, h])
            proj = jnp.dot(nrm[sec, h].reshape(HALF, D), wp[sec], preferred_element_type=F32)
            proj = silu(proj).astype(BF16)
            rows = slice(h * HALF, (h + 1) * HALF)
            seen = slice(0, (h + 1) * HALF)
            feats[rows] = proj
            gate, query = proj[:, :HD], proj[:, 2 * HD : 3 * HD]
            scores = lax.dot_general(
                query, feats[seen, 3 * HD :], (((1,), (1,)), ((), ())), preferred_element_type=F32
            ) * HD ** (-0.5)
            attn = (silu(scores) * mask[rows, seen]).astype(BF16)
            mixed = jnp.dot(attn, feats[seen, HD : 2 * HD], preferred_element_type=F32)
            mixed = mixed * lax.rsqrt(jnp.mean(mixed * mixed, axis=1, keepdims=True) + EPS)
            gated = (mixed * gate.astype(F32)).astype(BF16)
            back = jnp.dot(gated, wo[sec], preferred_element_type=F32).astype(BF16)
            part[sec, h] = back.reshape(MP, OWN, D)
            to_group(
                lambda to: part.at[sec, h, to], rsin.at[sec, h, m], rs_s.at[sec], rs_r.at[sec, h, m]
            )
        for h in range(2):
            acc = xrow[h] + part[sec, h, m].astype(F32)
            for d in (1, 3, 5, 7, 2, 6, 4):
                src = mp_peer(d)
                drain(rsin.at[sec, h, src], rs_r.at[sec, h, src])
                acc = acc + rsin[sec, h, src].astype(F32)
            new = acc.astype(BF16)
            if sec == 0:
                newf = new.astype(F32)
                xrow[h] = newf
                inv = lax.rsqrt(jnp.mean(newf * newf, axis=1, keepdims=True) + EPS)
                nrm[1, h, m] = (newf * inv * gbuf[1, 0:1, :]).astype(BF16)
                to_group(lambda to: nrm.at[1, h, m], nrm.at[1, h, m], ag_s.at[1], ag_r.at[1, h])
            else:
                states[h, m] = new
                to_group(lambda to: states.at[h, m], states.at[h, m], ag_s.at[2], ag_r.at[2, h])

    for h in range(2):
        drain(states.at[h, pl.ds(0, MP - 1)], ag_r.at[2, h])

    for copy in exchange:
        copy.wait_send()
    swap.wait_send()

    @pl.when(is_even)
    def _():
        drain(reqout.at[pl.ds(0, PEERS - 1)], req_s)
        drain(repout.at[pl.ds(0, PEERS - 1)], rep_s)

    @pl.when(p == 1)
    def _():
        drain(reqout, req_s)
        drain(repout, rep_s)

    for h in range(2):
        drain(xcols.at[h, pl.ds(0, MP - 1)], ag_s.at[0])
        drain(nrm.at[1, h, pl.ds(0, MP - 1)], ag_s.at[1])
        drain(states.at[h, pl.ds(0, MP - 1)], ag_s.at[2])
        for sec in range(2):
            drain(part.at[sec, h, pl.ds(0, MP - 1)], rs_s.at[sec])


def finish(states_ref, counts_ref, wctx_ref, bias_ref, out_hbm, ctx_ref, sem):
    write = pltpu.make_async_copy(states_ref, out_hbm, sem)
    write.start()
    scored = jnp.dot(
        states_ref[...].reshape(ROWS, D), wctx_ref[...], preferred_element_type=F32
    ).astype(BF16)
    summed = jnp.dot(counts_ref[...], scored, preferred_element_type=F32)
    ctx_ref[...] = silu(summed + bias_ref[...].astype(F32)).astype(BF16)
    write.wait()


def on_device(
    item_owner, item_row, segments, neighbors, table, gains, w_in, w_out, w_ctx, ctx_bias
):
    n_rows = item_row.shape[0]
    vmem = pl.BlockSpec(memory_space=pltpu.VMEM)
    hbm = pl.BlockSpec(memory_space=pltpu.HBM)
    dma = pltpu.SemaphoreType.DMA
    states, counts, wctx = pl.pallas_call(
        kernel,
        out_shape=(
            pltpu.VMEM((2, MP, OWN, D), BF16),
            pltpu.VMEM((ROWS, ROWS), BF16),
            pltpu.VMEM((D, HD), BF16),
        ),
        in_specs=[vmem] * 5 + [hbm] * 4,
        out_specs=(vmem, vmem, vmem),
        scratch_shapes=[
            pltpu.VMEM((D, HD), BF16),
            pltpu.VMEM((2, 4 * D, HD), BF16),
            pltpu.VMEM((2, D, 4 * HD), BF16),
            pltpu.VMEM((2, HD, D), BF16),
            pltpu.VMEM((2, 8, D), F32),
            pltpu.VMEM((PEERS, 1, HD), I32),
            pltpu.VMEM((PEERS, 1, HD), I32),
            pltpu.VMEM((PEERS, SLOTS, HD), BF16),
            pltpu.VMEM((PEERS, SLOTS, HD), BF16),
            pltpu.VMEM((2, ROWS, PEERS * SLOTS), BF16),
            pltpu.VMEM((2, ROWS, HD), BF16),
            pltpu.VMEM((ROWS, HD), BF16),
            pltpu.VMEM((2, MP, HALF, HD), BF16),
            pltpu.VMEM((ROWS, ROWS), F32),
            pltpu.VMEM((2, 2, MP, OWN, D), BF16),
            pltpu.VMEM((ROWS, 4 * HD), BF16),
            pltpu.VMEM((2, 2, MP, OWN, D), BF16),
            pltpu.VMEM((2, 2, MP, OWN, D), BF16),
            pltpu.VMEM((2, OWN, D), F32),
            dma((4,)),
            dma(()),
            dma(()),
            dma(()),
            dma(()),
            dma((3,)),
            dma((3,)),
            dma(()),
            dma(()),
            dma((3,)),
            dma((3, 2)),
            dma((2,)),
            dma((2, 2, MP)),
        ],
        compiler_params=pltpu.CompilerParams(
            collective_id=0, has_side_effects=True, vmem_limit_bytes=65700000
        ),
        name="cascade",
    )(
        item_owner.reshape(1, n_rows),
        item_row.reshape(1, n_rows),
        segments[0],
        jnp.swapaxes(neighbors[0], 1, 2),
        gains,
        table,
        w_in.reshape(4 * D, HD),
        w_out[0],
        w_ctx,
    )
    states, ctx = pl.pallas_call(
        finish,
        out_shape=(
            jax.ShapeDtypeStruct((2, MP, OWN, D), BF16),
            jax.ShapeDtypeStruct((ROWS, HD), BF16),
        ),
        in_specs=[vmem] * 4,
        out_specs=(hbm, vmem),
        scratch_shapes=[dma(())],
        compiler_params=pltpu.CompilerParams(vmem_limit_bytes=8 * 1024 * 1024),
        name="finish",
    )(states, counts, wctx, ctx_bias.reshape(1, -1))
    return states.reshape(1, 1, ROWS, D), ctx.reshape(1, 1, ROWS, HD)


def solution(mesh):
    in_specs = (
        P("dp", None),
        P("dp"),
        P("dp", None, None),
        P("dp", None, None, None),
        P("dp", None),
        P("phase", None),
        P("phase", None, None, "mp"),
        P("phase", "mp", None),
        P(None, "mp"),
        P("mp"),
    )
    out_specs = (P("dp", "phase", None, None), P("dp", "phase", None, "mp"))
    return jax.shard_map(
        on_device, mesh=mesh, in_specs=in_specs, out_specs=out_specs, check_vma=False
    )
```

```python
import functools

import jax
import jax.numpy as jnp
from jax import lax
from jax.experimental import pallas as pl
from jax.experimental.pallas import tpu as pltpu
from jax.sharding import PartitionSpec as P

MESH = pl.DeviceIdType.MESH
F32 = jnp.float32
BF16 = jnp.bfloat16
I32 = jnp.int32

D = 1024
HD = 128
NBR = 8
ROWS = 256
MP = 8
ZN = 12
YN = 4
PEERS = ZN // 2 * YN
SLOTS = 24
HALF = ROWS // 2
OWN = HALF // MP
EPS = 1e-06


def silu(x):
    half = 0.5 * x
    return half * (1.0 + jnp.tanh(half))


def iota(shape, axis):
    return lax.broadcasted_iota(I32, shape, axis)


def to_column(row):
    n = row.shape[1]
    diag = iota((n, n), 0) == iota((n, n), 1)
    return jnp.sum(jnp.where(diag, jnp.broadcast_to(row, (n, n)), 0.0), axis=1, keepdims=True)


def kernel(
    owner_ref, item_ref, seg_ref, nbr_ref, gain_ref, table_hbm, w_hbm, wo_hbm, wctx_hbm,
    states, counts, wctx,
    tcol, w4, wp, wo, gbuf, reqout, reqin, repout, repin, pick, part0, partin, xcols,
    mask, nrm, feats, part, rsin, xrow,
    loc, req_s, req_r, rep_s, rep_r, wex_s, wex_r, xp_s, xp_r, ag_s, ag_r, rs_s, rs_r,
):
    g = lax.axis_index("dp")
    m = lax.axis_index("mp")
    p = lax.axis_index("phase")
    q = 1 - p
    zg, yg = g // YN, g % YN
    slot_me = (zg // 2) * YN + yg
    is_even = p == 0

    m_y = lax.rem(m + MP // 2, MP)

    def dp_peer(j, dy):
        z = lax.rem(zg + 2 * j + p, ZN)
        y = lax.rem(yg + dy, YN)
        return (z * YN + y, m_y if dy == 2 else m, p), (z // 2) * YN + y

    def mp_peer(d):
        return lax.rem(m + d, MP)

    def remote(src, dst, s, r, dev):
        return pltpu.make_async_remote_copy(
            src_ref=src, dst_ref=dst, send_sem=s, recv_sem=r, device_id=dev, device_id_type=MESH
        )

    def drain(ref, sem):
        pltpu.make_async_copy(ref, ref, sem).wait()

    barrier = pltpu.get_barrier_semaphore()

    def greet(dev):
        pl.semaphore_signal(barrier, inc=1, device_id=dev, device_id_type=MESH)

    far_first = (3, 2, 4, 1, 5, 0)
    for j in far_first:
        for dy in (2, 1, 3, 0):
            dev, _ = dp_peer(j, dy)
            if (j, dy) == (0, 0):
                @pl.when(p == 1)
                def _():
                    greet(dev)
            else:
                greet(dev)
    for d in range(1, MP):
        greet((g, mp_peer(d), p))
    greet((g, m, q))

    col0 = pl.multiple_of(m * HD, HD)
    col1 = pl.multiple_of(m_y * HD, HD)
    loads = [
        pltpu.make_async_copy(table_hbm.at[:, pl.ds(col0, HD)], tcol.at[:, :HD], loc.at[0]),
        pltpu.make_async_copy(w_hbm, w4.at[p], loc.at[1]),
        pltpu.make_async_copy(wo_hbm, wo.at[p], loc.at[2]),
        pltpu.make_async_copy(table_hbm.at[:, pl.ds(col1, HD)], tcol.at[:, HD:], loc.at[4]),
    ]
    keep = pltpu.make_async_copy(wctx_hbm, wctx, loc.at[3])
    keep.start()
    for load in loads:
        load.start()
    gbuf[p] = jnp.broadcast_to(gain_ref[...].astype(F32), (8, D))

    n_rows = owner_ref.shape[1]
    owners = owner_ref[...]
    items = item_ref[...]
    slot_col = iota((PEERS, n_rows), 0)
    owner_of_slot = (2 * (slot_col // YN) + lax.rem(zg + p, 2)) * YN + slot_col % YN
    hit = (jnp.broadcast_to(owners, (PEERS, n_rows)) == owner_of_slot).astype(F32)
    before = (iota((n_rows, n_rows), 0) < iota((n_rows, n_rows), 1)).astype(F32).astype(BF16)
    count = jnp.dot(hit.astype(BF16), before, preferred_element_type=F32)
    rank = jnp.sum(hit * count, axis=0, keepdims=True)
    mine = jnp.sum(hit, axis=0, keepdims=True)
    slot_row = jnp.sum(hit * slot_col.astype(F32), axis=0, keepdims=True)
    key = jnp.where(mine > 0.5, slot_row * SLOTS + rank, -1.0)
    ranked = jnp.where(mine > 0.5, rank, -1.0)
    at_rank = (iota((HD, n_rows), 0).astype(F32) == jnp.broadcast_to(ranked, (HD, n_rows)))
    at_rank = at_rank.astype(F32).astype(BF16)
    hi = (items >> 5).astype(F32)
    lo = (items & 31).astype(F32)
    both = jnp.concatenate([hit * hi, hit * lo], axis=0).astype(BF16)
    found = lax.dot_general(both, at_rank, (((1,), (1,)), ((), ())), preferred_element_type=F32)
    wanted = (found[:PEERS] * 32.0 + found[PEERS:]).astype(I32)
    for s in range(PEERS):
        reqout[s] = wanted[s : s + 1]

    pl.semaphore_wait(barrier, 31 + p)

    def to_peers(src_of, dst, s_sem, r_sem, js):
        for j in js:
            seen_as = lax.rem(ZN // 2 - j - p, ZN // 2)
            for dy in (2, 1, 3, 0):
                dev, s = dp_peer(j, dy)
                if (j, dy) == (0, 0):
                    @pl.when(is_even)
                    def _():
                        pltpu.make_async_copy(
                            src_of.at[s], dst.at[slot_me], r_sem.at[seen_as]
                        ).start()

                    @pl.when(p == 1)
                    def _():
                        remote(
                            src_of.at[s], dst.at[slot_me], s_sem, r_sem.at[seen_as], dev
                        ).start()
                else:
                    remote(
                        src_of.at[s], dst.at[slot_me], s_sem, r_sem.at[seen_as], dev
                    ).start()

    def peers_at(j):
        return pl.ds((lax.rem(zg + 2 * j + p, ZN) // 2) * YN, YN)

    to_peers(reqout, reqin, req_s, req_r, far_first)

    loads[1].wait()
    loads[2].wait()
    sibling = (g, m, q)
    exchange = [
        remote(w4.at[p], w4.at[p], wex_s.at[0], wex_r.at[0], sibling),
        remote(wo.at[p], wo.at[p], wex_s.at[1], wex_r.at[1], sibling),
        remote(gbuf.at[p], gbuf.at[p], wex_s.at[2], wex_r.at[2], sibling),
    ]
    for copy in exchange:
        copy.start()

    per_chunk = 64
    src_col = iota((4 * per_chunk, 4 * per_chunk), 1)
    dst_row = iota((4 * per_chunk, 4 * per_chunk), 0)
    spread = (src_col == 4 * (dst_row % per_chunk) + dst_row // per_chunk).astype(F32).astype(BF16)

    def arrange(sec):
        def body(i, carry):
            base = pl.multiple_of(i * 4 * per_chunk, 4 * per_chunk)
            moved = jnp.dot(spread, w4[sec, pl.ds(base, 4 * per_chunk), :], preferred_element_type=F32)
            moved = moved.astype(BF16)
            to = pl.multiple_of(i * per_chunk, per_chunk)
            for c in range(4):
                wp[sec, pl.ds(to, per_chunk), c * HD : (c + 1) * HD] = moved[
                    c * per_chunk : (c + 1) * per_chunk
                ]
            return carry

        lax.fori_loop(0, D // per_chunk, body, 0, unroll=True)

    arrange(p)
    loads[0].wait()
    loads[3].wait()
    crossed = lax.rem(yg + 2, YN)
    for pair in ((0, 5), (1, 4), (2, 3)):
        columns = []
        for j in pair:
            drain(reqin.at[peers_at(j)], req_r.at[j])
            asked = jnp.broadcast_to(reqin[peers_at(j)], (YN, SLOTS, HD))
            on = iota((YN, SLOTS, HD), 1) == iota((YN, SLOTS, HD), 2)
            columns.append(
                jnp.sum(jnp.where(on, asked.astype(F32), 0.0), axis=2, keepdims=True).reshape(
                    YN * SLOTS, 1
                )
            )
        column = jnp.concatenate(columns, axis=0)
        size = 2 * YN * SLOTS
        hot = (column == iota((size, D), 1).astype(F32)).astype(F32).astype(BF16)
        rows = jnp.dot(hot, tcol[...], preferred_element_type=F32)
        group = (iota((size, HD), 0) // SLOTS) % YN
        rows = jnp.where(group == crossed, rows[:, HD:], rows[:, :HD]).astype(BF16)
        rows = rows.reshape(2, YN, SLOTS, HD)
        for i, j in enumerate(pair):
            repout[peers_at(j)] = rows[i]
        to_peers(repout, repin, rep_s, rep_r, pair[::-1])

    key_col = to_column(key)
    for h in range(2):
        lanes = iota((ROWS, PEERS * SLOTS), 1).astype(F32)
        pick[h] = (key_col[h * ROWS : (h + 1) * ROWS] == lanes).astype(F32).astype(BF16)

    exchange[0].wait_recv()
    exchange[1].wait_recv()
    exchange[2].wait_recv()
    arrange(q)
    seg = seg_ref[pl.ds(p, 1), :].astype(F32)
    seg_col = to_column(seg)
    below = iota((ROWS, ROWS), 1) <= iota((ROWS, ROWS), 0)
    same = seg_col == jnp.broadcast_to(seg, (ROWS, ROWS))
    mask[...] = jnp.where(below & same, 1.0 / ROWS, 0.0)
    hits = jnp.zeros((ROWS, ROWS), F32)
    near = nbr_ref[p]
    for n in range(NBR):
        row = jnp.broadcast_to(near[n : n + 1], (ROWS, ROWS))
        hits = hits + jnp.where(row == iota((ROWS, ROWS), 0), 1.0 / NBR, 0.0)
    counts[...] = hits.T.astype(BF16)
    keep.wait()

    for j in range(ZN // 2):
        drain(repin.at[peers_at(j)], rep_r.at[j])
    for h in range(2):
        part0[h] = jnp.dot(
            pick[h], repin[...].reshape(PEERS * SLOTS, HD), preferred_element_type=F32
        ).astype(BF16)
    swap = remote(part0.at[q], partin, xp_s, xp_r, sibling)
    swap.start()
    swap.wait_recv()
    own = part0[p] + partin[...]
    for h in range(2):
        xcols[h, m] = own[h * HALF : (h + 1) * HALF]

    def to_group(src_of, dst, s_sem, r_of):
        for d in (4, 2, 6, 5, 7, 1, 3):
            to = mp_peer(d)
            remote(src_of(to), dst, s_sem, r_of, (g, to, p)).start()

    for h in range(2):
        to_group(lambda to: xcols.at[h, m], xcols.at[h, m], ag_s.at[0], ag_r.at[0, h])

    own_row = pl.multiple_of(m * OWN, OWN)
    for sec in range(2):
        for h in range(2):
            if sec == 0:
                drain(xcols.at[h, pl.ds(0, MP - 1)], ag_r.at[0, h])
                total = jnp.zeros((HALF, 1), F32)
                for k in range(MP):
                    block = xcols[h, k].astype(F32)
                    total = total + jnp.sum(block * block, axis=1, keepdims=True)
                inv = lax.rsqrt(total * (1.0 / D) + EPS)
                for k in range(MP):
                    scaled = xcols[h, k].astype(F32) * inv * gbuf[0, 0:1, k * HD : (k + 1) * HD]
                    nrm[0, h, :, :, k * HD : (k + 1) * HD] = scaled.astype(BF16).reshape(MP, OWN, HD)
                    xrow[h, :, k * HD : (k + 1) * HD] = xcols[h, k, pl.ds(own_row, OWN), :].astype(F32)
            else:
                drain(nrm.at[1, h, pl.ds(0, MP - 1)], ag_r.at[1, h])
            proj = jnp.dot(nrm[sec, h].reshape(HALF, D), wp[sec], preferred_element_type=F32)
            proj = silu(proj).astype(BF16)
            rows = slice(h * HALF, (h + 1) * HALF)
            seen = slice(0, (h + 1) * HALF)
            feats[rows] = proj
            gate, query = proj[:, :HD], proj[:, 2 * HD : 3 * HD]
            scores = lax.dot_general(
                query, feats[seen, 3 * HD :], (((1,), (1,)), ((), ())), preferred_element_type=F32
            ) * HD ** (-0.5)
            attn = (silu(scores) * mask[rows, seen]).astype(BF16)
            mixed = jnp.dot(attn, feats[seen, HD : 2 * HD], preferred_element_type=F32)
            mixed = mixed * lax.rsqrt(jnp.mean(mixed * mixed, axis=1, keepdims=True) + EPS)
            gated = (mixed * gate.astype(F32)).astype(BF16)
            back = jnp.dot(gated, wo[sec], preferred_element_type=F32).astype(BF16)
            part[sec, h] = back.reshape(MP, OWN, D)
            to_group(
                lambda to: part.at[sec, h, to], rsin.at[sec, h, m], rs_s.at[sec], rs_r.at[sec, h, m]
            )
        for h in range(2):
            acc = xrow[h] + part[sec, h, m].astype(F32)
            for d in (1, 3, 5, 7, 2, 6, 4):
                src = mp_peer(d)
                drain(rsin.at[sec, h, src], rs_r.at[sec, h, src])
                acc = acc + rsin[sec, h, src].astype(F32)
            new = acc.astype(BF16)
            if sec == 0:
                newf = new.astype(F32)
                xrow[h] = newf
                inv = lax.rsqrt(jnp.mean(newf * newf, axis=1, keepdims=True) + EPS)
                nrm[1, h, m] = (newf * inv * gbuf[1, 0:1, :]).astype(BF16)
                to_group(lambda to: nrm.at[1, h, m], nrm.at[1, h, m], ag_s.at[1], ag_r.at[1, h])
            else:
                states[h, m] = new
                to_group(lambda to: states.at[h, m], states.at[h, m], ag_s.at[2], ag_r.at[2, h])

    for h in range(2):
        drain(states.at[h, pl.ds(0, MP - 1)], ag_r.at[2, h])

    for copy in exchange:
        copy.wait_send()
    swap.wait_send()

    @pl.when(is_even)
    def _():
        drain(reqout.at[pl.ds(0, PEERS - 1)], req_s)
        drain(repout.at[pl.ds(0, PEERS - 1)], rep_s)

    @pl.when(p == 1)
    def _():
        drain(reqout, req_s)
        drain(repout, rep_s)

    for h in range(2):
        drain(xcols.at[h, pl.ds(0, MP - 1)], ag_s.at[0])
        drain(nrm.at[1, h, pl.ds(0, MP - 1)], ag_s.at[1])
        drain(states.at[h, pl.ds(0, MP - 1)], ag_s.at[2])
        for sec in range(2):
            drain(part.at[sec, h, pl.ds(0, MP - 1)], rs_s.at[sec])


def finish(states_ref, counts_ref, wctx_ref, bias_ref, out_hbm, ctx_ref, sem):
    write = pltpu.make_async_copy(states_ref, out_hbm, sem)
    write.start()
    scored = jnp.dot(
        states_ref[...].reshape(ROWS, D), wctx_ref[...], preferred_element_type=F32
    ).astype(BF16)
    summed = jnp.dot(counts_ref[...], scored, preferred_element_type=F32)
    ctx_ref[...] = silu(summed + bias_ref[...].astype(F32)).astype(BF16)
    write.wait()


def on_device(
    item_owner, item_row, segments, neighbors, table, gains, w_in, w_out, w_ctx, ctx_bias
):
    n_rows = item_row.shape[0]
    vmem = pl.BlockSpec(memory_space=pltpu.VMEM)
    hbm = pl.BlockSpec(memory_space=pltpu.HBM)
    dma = pltpu.SemaphoreType.DMA
    states, counts, wctx = pl.pallas_call(
        kernel,
        out_shape=(
            pltpu.VMEM((2, MP, OWN, D), BF16),
            pltpu.VMEM((ROWS, ROWS), BF16),
            pltpu.VMEM((D, HD), BF16),
        ),
        in_specs=[vmem] * 5 + [hbm] * 4,
        out_specs=(vmem, vmem, vmem),
        scratch_shapes=[
            pltpu.VMEM((D, 2 * HD), BF16),
            pltpu.VMEM((2, 4 * D, HD), BF16),
            pltpu.VMEM((2, D, 4 * HD), BF16),
            pltpu.VMEM((2, HD, D), BF16),
            pltpu.VMEM((2, 8, D), F32),
            pltpu.VMEM((PEERS, 1, HD), I32),
            pltpu.VMEM((PEERS, 1, HD), I32),
            pltpu.VMEM((PEERS, SLOTS, HD), BF16),
            pltpu.VMEM((PEERS, SLOTS, HD), BF16),
            pltpu.VMEM((2, ROWS, PEERS * SLOTS), BF16),
            pltpu.VMEM((2, ROWS, HD), BF16),
            pltpu.VMEM((ROWS, HD), BF16),
            pltpu.VMEM((2, MP, HALF, HD), BF16),
            pltpu.VMEM((ROWS, ROWS), F32),
            pltpu.VMEM((2, 2, MP, OWN, D), BF16),
            pltpu.VMEM((ROWS, 4 * HD), BF16),
            pltpu.VMEM((2, 2, MP, OWN, D), BF16),
            pltpu.VMEM((2, 2, MP, OWN, D), BF16),
            pltpu.VMEM((2, OWN, D), F32),
            dma((5,)),
            dma(()),
            dma((ZN // 2,)),
            dma(()),
            dma((ZN // 2,)),
            dma((3,)),
            dma((3,)),
            dma(()),
            dma(()),
            dma((3,)),
            dma((3, 2)),
            dma((2,)),
            dma((2, 2, MP)),
        ],
        compiler_params=pltpu.CompilerParams(
            collective_id=0, has_side_effects=True, vmem_limit_bytes=65700000
        ),
        name="cascade",
    )(
        item_owner.reshape(1, n_rows),
        item_row.reshape(1, n_rows),
        segments[0],
        jnp.swapaxes(neighbors[0], 1, 2),
        gains,
        table,
        w_in.reshape(4 * D, HD),
        w_out[0],
        w_ctx,
    )
    states, ctx = pl.pallas_call(
        finish,
        out_shape=(
            jax.ShapeDtypeStruct((2, MP, OWN, D), BF16),
            jax.ShapeDtypeStruct((ROWS, HD), BF16),
        ),
        in_specs=[vmem] * 4,
        out_specs=(hbm, vmem),
        scratch_shapes=[dma(())],
        compiler_params=pltpu.CompilerParams(vmem_limit_bytes=8 * 1024 * 1024),
        name="finish",
    )(states, counts, wctx, ctx_bias.reshape(1, -1))
    return states.reshape(1, 1, ROWS, D), ctx.reshape(1, 1, ROWS, HD)


def solution(mesh):
    in_specs = (
        P("dp", None),
        P("dp"),
        P("dp", None, None),
        P("dp", None, None, None),
        P("dp", None),
        P("phase", None),
        P("phase", None, None, "mp"),
        P("phase", "mp", None),
        P(None, "mp"),
        P("mp"),
    )
    out_specs = (P("dp", "phase", None, None), P("dp", "phase", None, "mp"))
    return jax.shard_map(
        on_device, mesh=mesh, in_specs=in_specs, out_specs=out_specs, check_vma=False
    )
```

```python
import functools

import jax
import jax.numpy as jnp
from jax import lax
from jax.experimental import pallas as pl
from jax.experimental.pallas import tpu as pltpu
from jax.sharding import PartitionSpec as P

MESH = pl.DeviceIdType.MESH
F32 = jnp.float32
BF16 = jnp.bfloat16
I32 = jnp.int32

D = 1024
HD = 128
NBR = 8
ROWS = 256
MP = 8
ZN = 12
YN = 4
PEERS = ZN // 2 * YN
SLOTS = 18
HALF = ROWS // 2
OWN = HALF // MP
EPS = 1e-06


def silu(x):
    half = 0.5 * x
    return half * (1.0 + jnp.tanh(half))


def iota(shape, axis):
    return lax.broadcasted_iota(I32, shape, axis)


def to_column(row):
    n = row.shape[1]
    diag = iota((n, n), 0) == iota((n, n), 1)
    return jnp.sum(jnp.where(diag, jnp.broadcast_to(row, (n, n)), 0.0), axis=1, keepdims=True)


def kernel(
    owner_hbm, item_hbm, seg_hbm, nbr_hbm, gain_hbm, table_hbm, w_hbm, wo_hbm, wctx_hbm,
    states, counts, wctx,
    owner_ref, item_ref, seg_ref, nbr_ref, gain_ref,
    tcol, w4, wp, wo, gbuf, reqout, reqin, repout, repin, pick, part0, partin, xcols,
    mask, nrm, feats, part, rsin, xrow,
    loc, req_s, req_r, rep_s, rep_r, wex_s, wex_r, xp_s, xp_r, ag_s, ag_r, rs_s, rs_r,
):
    g = lax.axis_index("dp")
    m = lax.axis_index("mp")
    p = lax.axis_index("phase")
    q = 1 - p
    zg, yg = g // YN, g % YN
    slot_me = (zg // 2) * YN + yg
    is_even = p == 0

    m_y = lax.rem(m + MP // 2, MP)

    def dp_peer(j, dy):
        z = lax.rem(zg + 2 * j + p, ZN)
        y = lax.rem(yg + dy, YN)
        return (z * YN + y, m_y if dy == 2 else m, p), (z // 2) * YN + y

    def mp_peer(d):
        return lax.rem(m + d, MP)

    def remote(src, dst, s, r, dev):
        return pltpu.make_async_remote_copy(
            src_ref=src, dst_ref=dst, send_sem=s, recv_sem=r, device_id=dev, device_id_type=MESH
        )

    def drain(ref, sem):
        pltpu.make_async_copy(ref, ref, sem).wait()

    barrier = pltpu.get_barrier_semaphore()

    def greet(dev):
        pl.semaphore_signal(barrier, inc=1, device_id=dev, device_id_type=MESH)

    far_first = (3, 2, 4, 1, 5, 0)
    for j in far_first:
        for dy in (2, 1, 3, 0):
            dev, _ = dp_peer(j, dy)
            if (j, dy) == (0, 0):
                @pl.when(p == 1)
                def _():
                    greet(dev)
            else:
                greet(dev)
    for d in range(1, MP):
        greet((g, mp_peer(d), p))
    greet((g, m, q))

    col0 = pl.multiple_of(m * HD, HD)
    col1 = pl.multiple_of(m_y * HD, HD)
    loads = [
        pltpu.make_async_copy(table_hbm.at[:, pl.ds(col0, HD)], tcol.at[:, :HD], loc.at[0]),
        pltpu.make_async_copy(w_hbm, w4.at[p], loc.at[1]),
        pltpu.make_async_copy(wo_hbm, wo.at[p], loc.at[2]),
        pltpu.make_async_copy(table_hbm.at[:, pl.ds(col1, HD)], tcol.at[:, HD:], loc.at[4]),
    ]
    small = [
        pltpu.make_async_copy(owner_hbm, owner_ref, loc.at[5]),
        pltpu.make_async_copy(item_hbm, item_ref, loc.at[6]),
        pltpu.make_async_copy(gain_hbm, gain_ref, loc.at[7]),
        pltpu.make_async_copy(seg_hbm, seg_ref, loc.at[8]),
        pltpu.make_async_copy(nbr_hbm, nbr_ref, loc.at[9]),
    ]
    for load in small:
        load.start()
    keep = pltpu.make_async_copy(wctx_hbm, wctx, loc.at[3])
    keep.start()
    for load in loads:
        load.start()
    for load in small[:3]:
        load.wait()
    gbuf[p] = jnp.broadcast_to(gain_ref[...].astype(F32), (8, D))

    n_rows = owner_ref.shape[1]
    owners = owner_ref[...]
    items = item_ref[...]
    slot_col = iota((PEERS, n_rows), 0)
    owner_of_slot = (2 * (slot_col // YN) + lax.rem(zg + p, 2)) * YN + slot_col % YN
    hit = (jnp.broadcast_to(owners, (PEERS, n_rows)) == owner_of_slot).astype(F32)
    before = (iota((n_rows, n_rows), 0) < iota((n_rows, n_rows), 1)).astype(F32).astype(BF16)
    count = jnp.dot(hit.astype(BF16), before, preferred_element_type=F32)
    rank = jnp.sum(hit * count, axis=0, keepdims=True)
    mine = jnp.sum(hit, axis=0, keepdims=True)
    slot_row = jnp.sum(hit * slot_col.astype(F32), axis=0, keepdims=True)
    key = jnp.where(mine > 0.5, slot_row * SLOTS + rank, -1.0)
    ranked = jnp.where(mine > 0.5, rank, -1.0)
    at_rank = (iota((HD, n_rows), 0).astype(F32) == jnp.broadcast_to(ranked, (HD, n_rows)))
    at_rank = at_rank.astype(F32).astype(BF16)
    hi = (items >> 5).astype(F32)
    lo = (items & 31).astype(F32)
    both = jnp.concatenate([hit * hi, hit * lo], axis=0).astype(BF16)
    found = lax.dot_general(both, at_rank, (((1,), (1,)), ((), ())), preferred_element_type=F32)
    wanted = (found[:PEERS] * 32.0 + found[PEERS:]).astype(I32)
    for s in range(PEERS):
        reqout[s] = wanted[s : s + 1]

    pl.semaphore_wait(barrier, 31 + p)

    def to_peers(src_of, dst, s_sem, r_sem, js):
        for j in js:
            seen_as = lax.rem(ZN // 2 - j - p, ZN // 2)
            for dy in (2, 1, 3, 0):
                dev, s = dp_peer(j, dy)
                if (j, dy) == (0, 0):
                    @pl.when(is_even)
                    def _():
                        pltpu.make_async_copy(
                            src_of.at[s], dst.at[slot_me], r_sem.at[seen_as]
                        ).start()

                    @pl.when(p == 1)
                    def _():
                        remote(
                            src_of.at[s], dst.at[slot_me], s_sem, r_sem.at[seen_as], dev
                        ).start()
                else:
                    remote(
                        src_of.at[s], dst.at[slot_me], s_sem, r_sem.at[seen_as], dev
                    ).start()

    def peers_at(j):
        return pl.ds((lax.rem(zg + 2 * j + p, ZN) // 2) * YN, YN)

    to_peers(reqout, reqin, req_s, req_r, far_first)

    loads[1].wait()
    loads[2].wait()
    sibling = (g, m, q)
    exchange = [
        remote(w4.at[p], w4.at[p], wex_s.at[0], wex_r.at[0], sibling),
        remote(wo.at[p], wo.at[p], wex_s.at[1], wex_r.at[1], sibling),
        remote(gbuf.at[p], gbuf.at[p], wex_s.at[2], wex_r.at[2], sibling),
    ]
    for copy in exchange:
        copy.start()

    per_chunk = 64
    src_col = iota((4 * per_chunk, 4 * per_chunk), 1)
    dst_row = iota((4 * per_chunk, 4 * per_chunk), 0)
    spread = (src_col == 4 * (dst_row % per_chunk) + dst_row // per_chunk).astype(F32).astype(BF16)

    def arrange(sec):
        def body(i, carry):
            base = pl.multiple_of(i * 4 * per_chunk, 4 * per_chunk)
            moved = jnp.dot(spread, w4[sec, pl.ds(base, 4 * per_chunk), :], preferred_element_type=F32)
            moved = moved.astype(BF16)
            to = pl.multiple_of(i * per_chunk, per_chunk)
            for c in range(4):
                wp[sec, pl.ds(to, per_chunk), c * HD : (c + 1) * HD] = moved[
                    c * per_chunk : (c + 1) * per_chunk
                ]
            return carry

        lax.fori_loop(0, D // per_chunk, body, 0, unroll=True)

    arrange(p)
    loads[0].wait()
    loads[3].wait()
    crossed = lax.rem(yg + 2, YN)
    for pair in ((0, 5), (1, 4), (2, 3)):
        columns = []
        for j in pair:
            drain(reqin.at[peers_at(j)], req_r.at[j])
            asked = jnp.broadcast_to(reqin[peers_at(j)], (YN, 24, HD))
            on = iota((YN, 24, HD), 1) == iota((YN, 24, HD), 2)
            found = jnp.sum(jnp.where(on, asked.astype(F32), 0.0), axis=2, keepdims=True)
            columns.append(found[:, :SLOTS].reshape(YN * SLOTS, 1))
        column = jnp.concatenate(columns, axis=0)
        size = 2 * YN * SLOTS
        hot = (column == iota((size, D), 1).astype(F32)).astype(F32).astype(BF16)
        rows = jnp.dot(hot, tcol[...], preferred_element_type=F32)
        group = (iota((size, HD), 0) // SLOTS) % YN
        rows = jnp.where(group == crossed, rows[:, HD:], rows[:, :HD]).astype(BF16)
        rows = rows.reshape(2, YN, SLOTS // 2, 2, HD)
        for i, j in enumerate(pair):
            repout[peers_at(j)] = rows[i]
        to_peers(repout, repin, rep_s, rep_r, pair[::-1])

    key_col = to_column(key)
    for h in range(2):
        lanes = iota((ROWS, PEERS * SLOTS), 1).astype(F32)
        pick[h] = (key_col[h * ROWS : (h + 1) * ROWS] == lanes).astype(F32).astype(BF16)

    exchange[0].wait_recv()
    exchange[1].wait_recv()
    exchange[2].wait_recv()
    arrange(q)
    small[3].wait()
    small[4].wait()
    seg = seg_ref[pl.ds(p, 1), :].astype(F32)
    seg_col = to_column(seg)
    below = iota((ROWS, ROWS), 1) <= iota((ROWS, ROWS), 0)
    same = seg_col == jnp.broadcast_to(seg, (ROWS, ROWS))
    mask[...] = jnp.where(below & same, 1.0 / ROWS, 0.0)
    hits = jnp.zeros((ROWS, ROWS), F32)
    near = nbr_ref[p]
    for n in range(NBR):
        row = jnp.broadcast_to(near[n : n + 1], (ROWS, ROWS))
        hits = hits + jnp.where(row == iota((ROWS, ROWS), 0), 1.0 / NBR, 0.0)
    counts[...] = hits.T.astype(BF16)
    keep.wait()

    for j in range(ZN // 2):
        drain(repin.at[peers_at(j)], rep_r.at[j])
    def to_group(src_of, dst, s_sem, r_of):
        for d in (4, 2, 6, 5, 7, 1, 3):
            to = mp_peer(d)
            remote(src_of(to), dst, s_sem, r_of, (g, to, p)).start()

    halves = [slice(0, HALF), slice(HALF, ROWS)]
    rows = repin[...].reshape(PEERS * SLOTS, HD)
    swaps = []
    for h in range(2):
        theirs = jnp.dot(pick[q, halves[h]], rows, preferred_element_type=F32)
        part0[h] = theirs.astype(BF16)
        swaps.append(remote(part0.at[h], partin.at[h], xp_s.at[h], xp_r.at[h], sibling))
        swaps[h].start()
    mine = [
        jnp.dot(pick[p, halves[h]], rows, preferred_element_type=F32).astype(BF16)
        for h in range(2)
    ]
    for h in range(2):
        swaps[h].wait_recv()
        xcols[h, m] = mine[h] + partin[h]
        to_group(lambda to: xcols.at[h, m], xcols.at[h, m], ag_s.at[0], ag_r.at[0, h])

    own_row = pl.multiple_of(m * OWN, OWN)
    for sec in range(2):
        for h in range(2):
            if sec == 0:
                drain(xcols.at[h, pl.ds(0, MP - 1)], ag_r.at[0, h])
                total = jnp.zeros((HALF, 1), F32)
                for k in range(MP):
                    block = xcols[h, k].astype(F32)
                    total = total + jnp.sum(block * block, axis=1, keepdims=True)
                inv = lax.rsqrt(total * (1.0 / D) + EPS)
                for k in range(MP):
                    scaled = xcols[h, k].astype(F32) * inv * gbuf[0, 0:1, k * HD : (k + 1) * HD]
                    nrm[0, h, :, :, k * HD : (k + 1) * HD] = scaled.astype(BF16).reshape(MP, OWN, HD)
                    xrow[h, :, k * HD : (k + 1) * HD] = xcols[h, k, pl.ds(own_row, OWN), :].astype(F32)
            else:
                drain(nrm.at[1, h, pl.ds(0, MP - 1)], ag_r.at[1, h])
            proj = jnp.dot(nrm[sec, h].reshape(HALF, D), wp[sec], preferred_element_type=F32)
            proj = silu(proj).astype(BF16)
            rows = slice(h * HALF, (h + 1) * HALF)
            seen = slice(0, (h + 1) * HALF)
            feats[rows] = proj
            gate, query = proj[:, :HD], proj[:, 2 * HD : 3 * HD]
            scores = lax.dot_general(
                query, feats[seen, 3 * HD :], (((1,), (1,)), ((), ())), preferred_element_type=F32
            ) * HD ** (-0.5)
            attn = (silu(scores) * mask[rows, seen]).astype(BF16)
            mixed = jnp.dot(attn, feats[seen, HD : 2 * HD], preferred_element_type=F32)
            mixed = mixed * lax.rsqrt(jnp.mean(mixed * mixed, axis=1, keepdims=True) + EPS)
            gated = (mixed * gate.astype(F32)).astype(BF16)
            back = jnp.dot(gated, wo[sec], preferred_element_type=F32).astype(BF16)
            part[sec, h] = back.reshape(MP, OWN, D)
            to_group(
                lambda to: part.at[sec, h, to], rsin.at[sec, h, m], rs_s.at[sec], rs_r.at[sec, h, m]
            )
        for h in range(2):
            acc = xrow[h] + part[sec, h, m].astype(F32)
            for d in (1, 3, 5, 7, 2, 6, 4):
                src = mp_peer(d)
                drain(rsin.at[sec, h, src], rs_r.at[sec, h, src])
                acc = acc + rsin[sec, h, src].astype(F32)
            new = acc.astype(BF16)
            if sec == 0:
                newf = new.astype(F32)
                xrow[h] = newf
                inv = lax.rsqrt(jnp.mean(newf * newf, axis=1, keepdims=True) + EPS)
                nrm[1, h, m] = (newf * inv * gbuf[1, 0:1, :]).astype(BF16)
                to_group(lambda to: nrm.at[1, h, m], nrm.at[1, h, m], ag_s.at[1], ag_r.at[1, h])
            else:
                states[h, m] = new
                to_group(lambda to: states.at[h, m], states.at[h, m], ag_s.at[2], ag_r.at[2, h])

    for h in range(2):
        drain(states.at[h, pl.ds(0, MP - 1)], ag_r.at[2, h])

    for copy in exchange:
        copy.wait_send()
    for swap in swaps:
        swap.wait_send()

    @pl.when(is_even)
    def _():
        drain(reqout.at[pl.ds(0, PEERS - 1)], req_s)
        drain(repout.at[pl.ds(0, PEERS - 1)], rep_s)

    @pl.when(p == 1)
    def _():
        drain(reqout, req_s)
        drain(repout, rep_s)

    for h in range(2):
        drain(xcols.at[h, pl.ds(0, MP - 1)], ag_s.at[0])
        drain(nrm.at[1, h, pl.ds(0, MP - 1)], ag_s.at[1])
        drain(states.at[h, pl.ds(0, MP - 1)], ag_s.at[2])
        for sec in range(2):
            drain(part.at[sec, h, pl.ds(0, MP - 1)], rs_s.at[sec])


def finish(states_ref, counts_ref, wctx_ref, bias_ref, out_hbm, ctx_ref, sem):
    write = pltpu.make_async_copy(states_ref, out_hbm, sem)
    write.start()
    scored = jnp.dot(
        states_ref[...].reshape(ROWS, D), wctx_ref[...], preferred_element_type=F32
    ).astype(BF16)
    summed = jnp.dot(counts_ref[...], scored, preferred_element_type=F32)
    ctx_ref[...] = silu(summed + bias_ref[...].astype(F32)).astype(BF16)
    write.wait()


def on_device(
    item_owner, item_row, segments, neighbors, table, gains, w_in, w_out, w_ctx, ctx_bias
):
    n_rows = item_row.shape[0]
    vmem = pl.BlockSpec(memory_space=pltpu.VMEM)
    hbm = pl.BlockSpec(memory_space=pltpu.HBM)
    dma = pltpu.SemaphoreType.DMA
    states, counts, wctx = pl.pallas_call(
        kernel,
        out_shape=(
            pltpu.VMEM((2, MP, OWN, D), BF16),
            pltpu.VMEM((ROWS, ROWS), BF16),
            pltpu.VMEM((D, HD), BF16),
        ),
        in_specs=[hbm] * 9,
        out_specs=(vmem, vmem, vmem),
        scratch_shapes=[
            pltpu.VMEM((1, n_rows), I32),
            pltpu.VMEM((1, n_rows), I32),
            pltpu.VMEM((2, ROWS), I32),
            pltpu.VMEM((2, NBR, ROWS), I32),
            pltpu.VMEM((1, D), BF16),
            pltpu.VMEM((D, 2 * HD), BF16),
            pltpu.VMEM((2, 4 * D, HD), BF16),
            pltpu.VMEM((2, D, 4 * HD), BF16),
            pltpu.VMEM((2, HD, D), BF16),
            pltpu.VMEM((2, 8, D), F32),
            pltpu.VMEM((PEERS, 1, HD), I32),
            pltpu.VMEM((PEERS, 1, HD), I32),
            pltpu.VMEM((PEERS, SLOTS // 2, 2, HD), BF16),
            pltpu.VMEM((PEERS, SLOTS // 2, 2, HD), BF16),
            pltpu.VMEM((2, ROWS, PEERS * SLOTS), BF16),
            pltpu.VMEM((2, HALF, HD), BF16),
            pltpu.VMEM((2, HALF, HD), BF16),
            pltpu.VMEM((2, MP, HALF, HD), BF16),
            pltpu.VMEM((ROWS, ROWS), F32),
            pltpu.VMEM((2, 2, MP, OWN, D), BF16),
            pltpu.VMEM((ROWS, 4 * HD), BF16),
            pltpu.VMEM((2, 2, MP, OWN, D), BF16),
            pltpu.VMEM((2, 2, MP, OWN, D), BF16),
            pltpu.VMEM((2, OWN, D), F32),
            dma((10,)),
            dma(()),
            dma((ZN // 2,)),
            dma(()),
            dma((ZN // 2,)),
            dma((3,)),
            dma((3,)),
            dma((2,)),
            dma((2,)),
            dma((3,)),
            dma((3, 2)),
            dma((2,)),
            dma((2, 2, MP)),
        ],
        compiler_params=pltpu.CompilerParams(
            collective_id=0, has_side_effects=True, vmem_limit_bytes=65700000
        ),
        name="cascade",
    )(
        item_owner.reshape(1, n_rows),
        item_row.reshape(1, n_rows),
        segments[0],
        jnp.swapaxes(neighbors[0], 1, 2),
        gains,
        table,
        w_in.reshape(4 * D, HD),
        w_out[0],
        w_ctx,
    )
    states, ctx = pl.pallas_call(
        finish,
        out_shape=(
            jax.ShapeDtypeStruct((2, MP, OWN, D), BF16),
            jax.ShapeDtypeStruct((ROWS, HD), BF16),
        ),
        in_specs=[vmem] * 4,
        out_specs=(hbm, vmem),
        scratch_shapes=[dma(())],
        compiler_params=pltpu.CompilerParams(vmem_limit_bytes=8 * 1024 * 1024),
        name="finish",
    )(states, counts, wctx, ctx_bias.reshape(1, -1))
    return states.reshape(1, 1, ROWS, D), ctx.reshape(1, 1, ROWS, HD)


def solution(mesh):
    in_specs = (
        P("dp", None),
        P("dp"),
        P("dp", None, None),
        P("dp", None, None, None),
        P("dp", None),
        P("phase", None),
        P("phase", None, None, "mp"),
        P("phase", "mp", None),
        P(None, "mp"),
        P("mp"),
    )
    out_specs = (P("dp", "phase", None, None), P("dp", "phase", None, "mp"))
    return jax.shard_map(
        on_device, mesh=mesh, in_specs=in_specs, out_specs=out_specs, check_vma=False
    )
```

```python
import functools

import jax
import jax.numpy as jnp
from jax import lax
from jax.experimental import pallas as pl
from jax.experimental.pallas import tpu as pltpu
from jax.sharding import PartitionSpec as P

MESH = pl.DeviceIdType.MESH
F32 = jnp.float32
BF16 = jnp.bfloat16
I32 = jnp.int32

D = 1024
HD = 128
NBR = 8
ROWS = 256
MP = 8
ZN = 12
YN = 4
PEERS = ZN // 2 * YN
SLOTS = 18
HALF = ROWS // 2
OWN = HALF // MP
EPS = 1e-06


def silu(x):
    half = 0.5 * x
    return half * (1.0 + jnp.tanh(half))


def iota(shape, axis):
    return lax.broadcasted_iota(I32, shape, axis)


def to_column(row):
    n = row.shape[1]
    diag = iota((n, n), 0) == iota((n, n), 1)
    return jnp.sum(jnp.where(diag, jnp.broadcast_to(row, (n, n)), 0.0), axis=1, keepdims=True)


def kernel(
    owner_hbm, item_hbm, seg_hbm, nbr_hbm, gain_hbm, table_hbm, w_hbm, wo_hbm, wctx_hbm,
    states, counts, wctx, scored,
    owner_ref, item_ref, seg_ref, nbr_ref, gain_ref,
    tcol, w4, wp, wo, gbuf, reqout, reqin, repout, repin, pick, part0, partin, xcols,
    mask, nrm, feats, part, rsin, xrow,
    loc, req_s, req_r, rep_s, rep_r, wex_s, wex_r, xp_s, xp_r, ag_s, ag_r, rs_s, rs_r,
):
    g = lax.axis_index("dp")
    m = lax.axis_index("mp")
    p = lax.axis_index("phase")
    q = 1 - p
    zg, yg = g // YN, g % YN
    slot_me = (zg // 2) * YN + yg
    is_even = p == 0

    m_y = lax.rem(m + MP // 2, MP)

    def dp_peer(j, dy):
        z = lax.rem(zg + 2 * j + p, ZN)
        y = lax.rem(yg + dy, YN)
        return (z * YN + y, m_y if dy == 2 else m, p), (z // 2) * YN + y

    def mp_peer(d):
        return lax.rem(m + d, MP)

    def remote(src, dst, s, r, dev):
        return pltpu.make_async_remote_copy(
            src_ref=src, dst_ref=dst, send_sem=s, recv_sem=r, device_id=dev, device_id_type=MESH
        )

    def drain(ref, sem):
        pltpu.make_async_copy(ref, ref, sem).wait()

    barrier = pltpu.get_barrier_semaphore()

    def greet(dev):
        pl.semaphore_signal(barrier, inc=1, device_id=dev, device_id_type=MESH)

    far_first = (3, 2, 4, 1, 5, 0)
    for j in far_first:
        for dy in (2, 1, 3, 0):
            dev, _ = dp_peer(j, dy)
            if (j, dy) == (0, 0):
                @pl.when(p == 1)
                def _():
                    greet(dev)
            else:
                greet(dev)
    for d in range(1, MP):
        greet((g, mp_peer(d), p))
    greet((g, m, q))

    col0 = pl.multiple_of(m * HD, HD)
    col1 = pl.multiple_of(m_y * HD, HD)
    loads = [
        pltpu.make_async_copy(table_hbm.at[:, pl.ds(col0, HD)], tcol.at[:, :HD], loc.at[0]),
        pltpu.make_async_copy(w_hbm, w4.at[p], loc.at[1]),
        pltpu.make_async_copy(wo_hbm, wo.at[p], loc.at[2]),
        pltpu.make_async_copy(table_hbm.at[:, pl.ds(col1, HD)], tcol.at[:, HD:], loc.at[4]),
    ]
    small = [
        pltpu.make_async_copy(owner_hbm, owner_ref, loc.at[5]),
        pltpu.make_async_copy(item_hbm, item_ref, loc.at[6]),
        pltpu.make_async_copy(gain_hbm, gain_ref, loc.at[7]),
        pltpu.make_async_copy(seg_hbm, seg_ref, loc.at[8]),
        pltpu.make_async_copy(nbr_hbm, nbr_ref, loc.at[9]),
    ]
    for load in small:
        load.start()
    keep = pltpu.make_async_copy(wctx_hbm, wctx, loc.at[3])
    keep.start()
    for load in loads:
        load.start()
    for load in small[:3]:
        load.wait()
    gbuf[p] = jnp.broadcast_to(gain_ref[...].astype(F32), (8, D))

    n_rows = owner_ref.shape[1]
    owners = owner_ref[...]
    items = item_ref[...]
    slot_col = iota((PEERS, n_rows), 0)
    owner_of_slot = (2 * (slot_col // YN) + lax.rem(zg + p, 2)) * YN + slot_col % YN
    hit = (jnp.broadcast_to(owners, (PEERS, n_rows)) == owner_of_slot).astype(F32)
    before = (iota((n_rows, n_rows), 0) < iota((n_rows, n_rows), 1)).astype(F32).astype(BF16)
    count = jnp.dot(hit.astype(BF16), before, preferred_element_type=F32)
    rank = jnp.sum(hit * count, axis=0, keepdims=True)
    mine = jnp.sum(hit, axis=0, keepdims=True)
    slot_row = jnp.sum(hit * slot_col.astype(F32), axis=0, keepdims=True)
    key = jnp.where(mine > 0.5, slot_row * SLOTS + rank, -1.0)
    ranked = jnp.where(mine > 0.5, rank, -1.0)
    at_rank = (iota((HD, n_rows), 0).astype(F32) == jnp.broadcast_to(ranked, (HD, n_rows)))
    at_rank = at_rank.astype(F32).astype(BF16)
    hi = (items >> 5).astype(F32)
    lo = (items & 31).astype(F32)
    both = jnp.concatenate([hit * hi, hit * lo], axis=0).astype(BF16)
    found = lax.dot_general(both, at_rank, (((1,), (1,)), ((), ())), preferred_element_type=F32)
    wanted = (found[:PEERS] * 32.0 + found[PEERS:]).astype(I32)
    for s in range(PEERS):
        reqout[s] = wanted[s : s + 1]

    pl.semaphore_wait(barrier, 31 + p)

    def to_peers(src_of, dst, s_sem, r_sem, js):
        for j in js:
            seen_as = lax.rem(ZN // 2 - j - p, ZN // 2)
            for dy in (2, 1, 3, 0):
                dev, s = dp_peer(j, dy)
                if (j, dy) == (0, 0):
                    @pl.when(is_even)
                    def _():
                        pltpu.make_async_copy(
                            src_of.at[s], dst.at[slot_me], r_sem.at[seen_as]
                        ).start()

                    @pl.when(p == 1)
                    def _():
                        remote(
                            src_of.at[s], dst.at[slot_me], s_sem, r_sem.at[seen_as], dev
                        ).start()
                else:
                    remote(
                        src_of.at[s], dst.at[slot_me], s_sem, r_sem.at[seen_as], dev
                    ).start()

    def peers_at(j):
        return pl.ds((lax.rem(zg + 2 * j + p, ZN) // 2) * YN, YN)

    to_peers(reqout, reqin, req_s, req_r, far_first)

    loads[1].wait()
    loads[2].wait()
    sibling = (g, m, q)
    exchange = [
        remote(w4.at[p], w4.at[p], wex_s.at[0], wex_r.at[0], sibling),
        remote(wo.at[p], wo.at[p], wex_s.at[1], wex_r.at[1], sibling),
        remote(gbuf.at[p], gbuf.at[p], wex_s.at[2], wex_r.at[2], sibling),
    ]
    for copy in exchange:
        copy.start()

    per_chunk = 64
    src_col = iota((4 * per_chunk, 4 * per_chunk), 1)
    dst_row = iota((4 * per_chunk, 4 * per_chunk), 0)
    spread = (src_col == 4 * (dst_row % per_chunk) + dst_row // per_chunk).astype(F32).astype(BF16)

    def arrange(sec):
        def body(i, carry):
            base = pl.multiple_of(i * 4 * per_chunk, 4 * per_chunk)
            moved = jnp.dot(spread, w4[sec, pl.ds(base, 4 * per_chunk), :], preferred_element_type=F32)
            moved = moved.astype(BF16)
            to = pl.multiple_of(i * per_chunk, per_chunk)
            for c in range(4):
                wp[sec, pl.ds(to, per_chunk), c * HD : (c + 1) * HD] = moved[
                    c * per_chunk : (c + 1) * per_chunk
                ]
            return carry

        lax.fori_loop(0, D // per_chunk, body, 0, unroll=True)

    arrange(p)
    loads[0].wait()
    loads[3].wait()
    crossed = lax.rem(yg + 2, YN)
    for pair in ((0, 5), (1, 4), (2, 3)):
        columns = []
        for j in pair:
            drain(reqin.at[peers_at(j)], req_r.at[j])
            asked = jnp.broadcast_to(reqin[peers_at(j)], (YN, 24, HD))
            on = iota((YN, 24, HD), 1) == iota((YN, 24, HD), 2)
            found = jnp.sum(jnp.where(on, asked.astype(F32), 0.0), axis=2, keepdims=True)
            columns.append(found[:, :SLOTS].reshape(YN * SLOTS, 1))
        column = jnp.concatenate(columns, axis=0)
        size = 2 * YN * SLOTS
        hot = (column == iota((size, D), 1).astype(F32)).astype(F32).astype(BF16)
        rows = jnp.dot(hot, tcol[...], preferred_element_type=F32)
        group = (iota((size, HD), 0) // SLOTS) % YN
        rows = jnp.where(group == crossed, rows[:, HD:], rows[:, :HD]).astype(BF16)
        rows = rows.reshape(2, YN, SLOTS // 2, 2, HD)
        for i, j in enumerate(pair):
            repout[peers_at(j)] = rows[i]
        to_peers(repout, repin, rep_s, rep_r, pair[::-1])

    key_col = to_column(key)
    for h in range(2):
        lanes = iota((ROWS, PEERS * SLOTS), 1).astype(F32)
        pick[h] = (key_col[h * ROWS : (h + 1) * ROWS] == lanes).astype(F32).astype(BF16)

    exchange[0].wait_recv()
    exchange[1].wait_recv()
    exchange[2].wait_recv()
    arrange(q)
    small[3].wait()
    small[4].wait()
    seg = seg_ref[pl.ds(p, 1), :].astype(F32)
    seg_col = to_column(seg)
    below = iota((ROWS, ROWS), 1) <= iota((ROWS, ROWS), 0)
    same = seg_col == jnp.broadcast_to(seg, (ROWS, ROWS))
    mask[...] = jnp.where(below & same, 1.0 / ROWS, 0.0)
    hits = jnp.zeros((ROWS, ROWS), F32)
    near = nbr_ref[p]
    for n in range(NBR):
        row = jnp.broadcast_to(near[n : n + 1], (ROWS, ROWS))
        hits = hits + jnp.where(row == iota((ROWS, ROWS), 0), 1.0 / NBR, 0.0)
    counts[...] = hits.T.astype(BF16)
    keep.wait()

    for j in range(ZN // 2):
        drain(repin.at[peers_at(j)], rep_r.at[j])
    def to_group(src_of, dst, s_sem, r_of):
        for d in (4, 2, 6, 5, 7, 1, 3):
            to = mp_peer(d)
            remote(src_of(to), dst, s_sem, r_of, (g, to, p)).start()

    halves = [slice(0, HALF), slice(HALF, ROWS)]
    rows = repin[...].reshape(PEERS * SLOTS, HD)
    swaps = []
    for h in range(2):
        theirs = jnp.dot(pick[q, halves[h]], rows, preferred_element_type=F32)
        part0[h] = theirs.astype(BF16)
        swaps.append(remote(part0.at[h], partin.at[h], xp_s.at[h], xp_r.at[h], sibling))
        swaps[h].start()
    mine = [
        jnp.dot(pick[p, halves[h]], rows, preferred_element_type=F32).astype(BF16)
        for h in range(2)
    ]
    for h in range(2):
        swaps[h].wait_recv()
        xcols[h, m] = mine[h] + partin[h]
        to_group(lambda to: xcols.at[h, m], xcols.at[h, m], ag_s.at[0], ag_r.at[0, h])

    own_row = pl.multiple_of(m * OWN, OWN)
    for sec in range(2):
        for h in range(2):
            if sec == 0:
                drain(xcols.at[h, pl.ds(0, MP - 1)], ag_r.at[0, h])
                total = jnp.zeros((HALF, 1), F32)
                for k in range(MP):
                    block = xcols[h, k].astype(F32)
                    total = total + jnp.sum(block * block, axis=1, keepdims=True)
                inv = lax.rsqrt(total * (1.0 / D) + EPS)
                for k in range(MP):
                    scaled = xcols[h, k].astype(F32) * inv * gbuf[0, 0:1, k * HD : (k + 1) * HD]
                    nrm[0, h, :, :, k * HD : (k + 1) * HD] = scaled.astype(BF16).reshape(MP, OWN, HD)
                    xrow[h, :, k * HD : (k + 1) * HD] = xcols[h, k, pl.ds(own_row, OWN), :].astype(F32)
            else:
                drain(nrm.at[1, h, pl.ds(0, MP - 1)], ag_r.at[1, h])
            proj = jnp.dot(nrm[sec, h].reshape(HALF, D), wp[sec], preferred_element_type=F32)
            proj = silu(proj).astype(BF16)
            rows = slice(h * HALF, (h + 1) * HALF)
            seen = slice(0, (h + 1) * HALF)
            feats[rows] = proj
            gate, query = proj[:, :HD], proj[:, 2 * HD : 3 * HD]
            scores = lax.dot_general(
                query, feats[seen, 3 * HD :], (((1,), (1,)), ((), ())), preferred_element_type=F32
            ) * HD ** (-0.5)
            attn = (silu(scores) * mask[rows, seen]).astype(BF16)
            mixed = jnp.dot(attn, feats[seen, HD : 2 * HD], preferred_element_type=F32)
            mixed = mixed * lax.rsqrt(jnp.mean(mixed * mixed, axis=1, keepdims=True) + EPS)
            gated = (mixed * gate.astype(F32)).astype(BF16)
            back = jnp.dot(gated, wo[sec], preferred_element_type=F32).astype(BF16)
            part[sec, h] = back.reshape(MP, OWN, D)
            to_group(
                lambda to: part.at[sec, h, to], rsin.at[sec, h, m], rs_s.at[sec], rs_r.at[sec, h, m]
            )
        for h in range(2):
            acc = xrow[h] + part[sec, h, m].astype(F32)
            for d in (1, 3, 5, 7, 2, 6, 4):
                src = mp_peer(d)
                drain(rsin.at[sec, h, src], rs_r.at[sec, h, src])
                acc = acc + rsin[sec, h, src].astype(F32)
            new = acc.astype(BF16)
            if sec == 0:
                newf = new.astype(F32)
                xrow[h] = newf
                inv = lax.rsqrt(jnp.mean(newf * newf, axis=1, keepdims=True) + EPS)
                nrm[1, h, m] = (newf * inv * gbuf[1, 0:1, :]).astype(BF16)
                to_group(lambda to: nrm.at[1, h, m], nrm.at[1, h, m], ag_s.at[1], ag_r.at[1, h])
            else:
                states[h, m] = new
                to_group(lambda to: states.at[h, m], states.at[h, m], ag_s.at[2], ag_r.at[2, h])

    drain(states.at[0, pl.ds(0, MP - 1)], ag_r.at[2, 0])
    scored[...] = jnp.dot(
        states[0].reshape(HALF, D), wctx[...], preferred_element_type=F32
    ).astype(BF16)
    drain(states.at[1, pl.ds(0, MP - 1)], ag_r.at[2, 1])

    for copy in exchange:
        copy.wait_send()
    for swap in swaps:
        swap.wait_send()

    @pl.when(is_even)
    def _():
        drain(reqout.at[pl.ds(0, PEERS - 1)], req_s)
        drain(repout.at[pl.ds(0, PEERS - 1)], rep_s)

    @pl.when(p == 1)
    def _():
        drain(reqout, req_s)
        drain(repout, rep_s)

    for h in range(2):
        drain(xcols.at[h, pl.ds(0, MP - 1)], ag_s.at[0])
        drain(nrm.at[1, h, pl.ds(0, MP - 1)], ag_s.at[1])
        drain(states.at[h, pl.ds(0, MP - 1)], ag_s.at[2])
        for sec in range(2):
            drain(part.at[sec, h, pl.ds(0, MP - 1)], rs_s.at[sec])


def finish(
    states_ref, counts_ref, wctx_ref, scored_ref, bias_ref, out_hbm, ctx_hbm, ctx_ref, sem
):
    writes = [
        pltpu.make_async_copy(states_ref.at[h], out_hbm.at[h], sem.at[h]) for h in range(2)
    ]
    for write in writes:
        write.start()
    rest = jnp.dot(
        states_ref[1].reshape(HALF, D), wctx_ref[...], preferred_element_type=F32
    ).astype(BF16)
    summed = jnp.dot(counts_ref[:, :HALF], scored_ref[...], preferred_element_type=F32)
    summed = summed + jnp.dot(counts_ref[:, HALF:], rest, preferred_element_type=F32)
    ctx_ref[...] = silu(summed + bias_ref[...].astype(F32)).astype(BF16)
    writes.append(pltpu.make_async_copy(ctx_ref, ctx_hbm, sem.at[2]))
    writes[2].start()
    for write in writes:
        write.wait()


def on_device(
    item_owner, item_row, segments, neighbors, table, gains, w_in, w_out, w_ctx, ctx_bias
):
    n_rows = item_row.shape[0]
    vmem = pl.BlockSpec(memory_space=pltpu.VMEM)
    hbm = pl.BlockSpec(memory_space=pltpu.HBM)
    dma = pltpu.SemaphoreType.DMA
    states, counts, wctx, scored = pl.pallas_call(
        kernel,
        out_shape=(
            pltpu.VMEM((2, MP, OWN, D), BF16),
            pltpu.VMEM((ROWS, ROWS), BF16),
            pltpu.VMEM((D, HD), BF16),
            pltpu.VMEM((HALF, HD), BF16),
        ),
        in_specs=[hbm] * 9,
        out_specs=(vmem, vmem, vmem, vmem),
        scratch_shapes=[
            pltpu.VMEM((1, n_rows), I32),
            pltpu.VMEM((1, n_rows), I32),
            pltpu.VMEM((2, ROWS), I32),
            pltpu.VMEM((2, NBR, ROWS), I32),
            pltpu.VMEM((1, D), BF16),
            pltpu.VMEM((D, 2 * HD), BF16),
            pltpu.VMEM((2, 4 * D, HD), BF16),
            pltpu.VMEM((2, D, 4 * HD), BF16),
            pltpu.VMEM((2, HD, D), BF16),
            pltpu.VMEM((2, 8, D), F32),
            pltpu.VMEM((PEERS, 1, HD), I32),
            pltpu.VMEM((PEERS, 1, HD), I32),
            pltpu.VMEM((PEERS, SLOTS // 2, 2, HD), BF16),
            pltpu.VMEM((PEERS, SLOTS // 2, 2, HD), BF16),
            pltpu.VMEM((2, ROWS, PEERS * SLOTS), BF16),
            pltpu.VMEM((2, HALF, HD), BF16),
            pltpu.VMEM((2, HALF, HD), BF16),
            pltpu.VMEM((2, MP, HALF, HD), BF16),
            pltpu.VMEM((ROWS, ROWS), F32),
            pltpu.VMEM((2, 2, MP, OWN, D), BF16),
            pltpu.VMEM((ROWS, 4 * HD), BF16),
            pltpu.VMEM((2, 2, MP, OWN, D), BF16),
            pltpu.VMEM((2, 2, MP, OWN, D), BF16),
            pltpu.VMEM((2, OWN, D), F32),
            dma((10,)),
            dma(()),
            dma((ZN // 2,)),
            dma(()),
            dma((ZN // 2,)),
            dma((3,)),
            dma((3,)),
            dma((2,)),
            dma((2,)),
            dma((3,)),
            dma((3, 2)),
            dma((2,)),
            dma((2, 2, MP)),
        ],
        compiler_params=pltpu.CompilerParams(
            collective_id=0, has_side_effects=True, vmem_limit_bytes=65700000
        ),
        name="cascade",
    )(
        item_owner.reshape(1, n_rows),
        item_row.reshape(1, n_rows),
        segments[0],
        jnp.swapaxes(neighbors[0], 1, 2),
        gains,
        table,
        w_in.reshape(4 * D, HD),
        w_out[0],
        w_ctx,
    )
    states, ctx = pl.pallas_call(
        finish,
        out_shape=(
            jax.ShapeDtypeStruct((2, MP, OWN, D), BF16),
            jax.ShapeDtypeStruct((ROWS, HD), BF16),
        ),
        in_specs=[vmem] * 5,
        out_specs=(hbm, hbm),
        scratch_shapes=[pltpu.VMEM((ROWS, HD), BF16), dma((3,))],
        compiler_params=pltpu.CompilerParams(vmem_limit_bytes=8 * 1024 * 1024),
        name="finish",
    )(states, counts, wctx, scored, ctx_bias.reshape(1, -1))
    return states.reshape(1, 1, ROWS, D), ctx.reshape(1, 1, ROWS, HD)


def solution(mesh):
    in_specs = (
        P("dp", None),
        P("dp"),
        P("dp", None, None),
        P("dp", None, None, None),
        P("dp", None),
        P("phase", None),
        P("phase", None, None, "mp"),
        P("phase", "mp", None),
        P(None, "mp"),
        P("mp"),
    )
    out_specs = (P("dp", "phase", None, None), P("dp", "phase", None, "mp"))
    return jax.shard_map(
        on_device, mesh=mesh, in_specs=in_specs, out_specs=out_specs, check_vma=False
    )
```

```python
import functools

import jax
import jax.numpy as jnp
from jax import lax
from jax.experimental import pallas as pl
from jax.experimental.pallas import tpu as pltpu
from jax.sharding import PartitionSpec as P

MESH = pl.DeviceIdType.MESH
F32 = jnp.float32
BF16 = jnp.bfloat16
I32 = jnp.int32

D = 1024
HD = 128
NBR = 8
ROWS = 256
MP = 8
ZN = 12
YN = 4
PEERS = ZN // 2 * YN
SLOTS = 18
HALF = ROWS // 2
OWN = HALF // MP
EPS = 1e-06


def silu(x):
    half = 0.5 * x
    return half * (1.0 + jnp.tanh(half))


def iota(shape, axis):
    return lax.broadcasted_iota(I32, shape, axis)


def to_column(row):
    n = row.shape[1]
    diag = iota((n, n), 0) == iota((n, n), 1)
    return jnp.sum(jnp.where(diag, jnp.broadcast_to(row, (n, n)), 0.0), axis=1, keepdims=True)


def kernel(
    owner_hbm, item_hbm, seg_hbm, nbr_hbm, gain_hbm, table_hbm, w_hbm, wo_hbm, wctx_hbm,
    states, counts, wctx, scored,
    owner_ref, item_ref, seg_ref, nbr_ref, gain_ref,
    tcol, w4, wp, wo, gbuf, reqout, reqin, repout, repin, pick, part0, partin, xcols,
    mask, nrm, feats, part, rsin, xrow,
    loc, req_s, req_r, rep_s, rep_r, wex_s, wex_r, xp_s, xp_r, ag_s, ag_r, rs_s, rs_r, fin_r,
):
    g = lax.axis_index("dp")
    m = lax.axis_index("mp")
    p = lax.axis_index("phase")
    q = 1 - p
    zg, yg = g // YN, g % YN
    slot_me = (zg // 2) * YN + yg
    is_even = p == 0

    m_y = lax.rem(m + MP // 2, MP)

    def dp_peer(j, dy):
        z = lax.rem(zg + 2 * j + p, ZN)
        y = lax.rem(yg + dy, YN)
        return (z * YN + y, m_y if dy == 2 else m, p), (z // 2) * YN + y

    def mp_peer(d):
        return lax.rem(m + d, MP)

    def remote(src, dst, s, r, dev):
        return pltpu.make_async_remote_copy(
            src_ref=src, dst_ref=dst, send_sem=s, recv_sem=r, device_id=dev, device_id_type=MESH
        )

    def drain(ref, sem):
        pltpu.make_async_copy(ref, ref, sem).wait()

    barrier = pltpu.get_barrier_semaphore()

    def greet(dev):
        pl.semaphore_signal(barrier, inc=1, device_id=dev, device_id_type=MESH)

    far_first = (3, 2, 4, 1, 5, 0)
    for j in far_first:
        for dy in (2, 1, 3, 0):
            dev, _ = dp_peer(j, dy)
            if (j, dy) == (0, 0):
                @pl.when(p == 1)
                def _():
                    greet(dev)
            else:
                greet(dev)
    for d in range(1, MP):
        greet((g, mp_peer(d), p))
    greet((g, m, q))

    col0 = pl.multiple_of(m * HD, HD)
    col1 = pl.multiple_of(m_y * HD, HD)
    loads = [
        pltpu.make_async_copy(table_hbm.at[:, pl.ds(col0, HD)], tcol.at[:, :HD], loc.at[0]),
        pltpu.make_async_copy(w_hbm, w4.at[p], loc.at[1]),
        pltpu.make_async_copy(wo_hbm, wo.at[p], loc.at[2]),
        pltpu.make_async_copy(table_hbm.at[:, pl.ds(col1, HD)], tcol.at[:, HD:], loc.at[4]),
    ]
    small = [
        pltpu.make_async_copy(owner_hbm, owner_ref, loc.at[5]),
        pltpu.make_async_copy(item_hbm, item_ref, loc.at[6]),
        pltpu.make_async_copy(gain_hbm, gain_ref, loc.at[7]),
        pltpu.make_async_copy(seg_hbm, seg_ref, loc.at[8]),
        pltpu.make_async_copy(nbr_hbm, nbr_ref, loc.at[9]),
    ]
    for load in small:
        load.start()
    keep = pltpu.make_async_copy(wctx_hbm, wctx, loc.at[3])
    keep.start()
    for load in loads:
        load.start()
    for load in small[:3]:
        load.wait()
    gbuf[p] = jnp.broadcast_to(gain_ref[...].astype(F32), (8, D))

    n_rows = owner_ref.shape[1]
    owners = owner_ref[...]
    items = item_ref[...]
    slot_col = iota((PEERS, n_rows), 0)
    owner_of_slot = (2 * (slot_col // YN) + lax.rem(zg + p, 2)) * YN + slot_col % YN
    hit = (jnp.broadcast_to(owners, (PEERS, n_rows)) == owner_of_slot).astype(F32)
    before = (iota((n_rows, n_rows), 0) < iota((n_rows, n_rows), 1)).astype(F32).astype(BF16)
    count = jnp.dot(hit.astype(BF16), before, preferred_element_type=F32)
    rank = jnp.sum(hit * count, axis=0, keepdims=True)
    mine = jnp.sum(hit, axis=0, keepdims=True)
    slot_row = jnp.sum(hit * slot_col.astype(F32), axis=0, keepdims=True)
    key = jnp.where(mine > 0.5, slot_row * SLOTS + rank, -1.0)
    ranked = jnp.where(mine > 0.5, rank, -1.0)
    at_rank = (iota((HD, n_rows), 0).astype(F32) == jnp.broadcast_to(ranked, (HD, n_rows)))
    at_rank = at_rank.astype(F32).astype(BF16)
    hi = (items >> 5).astype(F32)
    lo = (items & 31).astype(F32)
    both = jnp.concatenate([hit * hi, hit * lo], axis=0).astype(BF16)
    found = lax.dot_general(both, at_rank, (((1,), (1,)), ((), ())), preferred_element_type=F32)
    wanted = (found[:PEERS] * 32.0 + found[PEERS:]).astype(I32)
    for s in range(PEERS):
        reqout[s] = wanted[s : s + 1]

    pl.semaphore_wait(barrier, 31 + p)

    def to_peers(src_of, dst, s_sem, r_sem, js):
        for j in js:
            seen_as = lax.rem(ZN // 2 - j - p, ZN // 2)
            for dy in (2, 1, 3, 0):
                dev, s = dp_peer(j, dy)
                if (j, dy) == (0, 0):
                    @pl.when(is_even)
                    def _():
                        pltpu.make_async_copy(
                            src_of.at[s], dst.at[slot_me], r_sem.at[seen_as]
                        ).start()

                    @pl.when(p == 1)
                    def _():
                        remote(
                            src_of.at[s], dst.at[slot_me], s_sem, r_sem.at[seen_as], dev
                        ).start()
                else:
                    remote(
                        src_of.at[s], dst.at[slot_me], s_sem, r_sem.at[seen_as], dev
                    ).start()

    def peers_at(j):
        return pl.ds((lax.rem(zg + 2 * j + p, ZN) // 2) * YN, YN)

    to_peers(reqout, reqin, req_s, req_r, far_first)

    loads[1].wait()
    loads[2].wait()
    sibling = (g, m, q)
    exchange = [
        remote(w4.at[p], w4.at[p], wex_s.at[0], wex_r.at[0], sibling),
        remote(wo.at[p], wo.at[p], wex_s.at[1], wex_r.at[1], sibling),
        remote(gbuf.at[p], gbuf.at[p], wex_s.at[2], wex_r.at[2], sibling),
    ]
    for copy in exchange:
        copy.start()

    per_chunk = 64
    src_col = iota((4 * per_chunk, 4 * per_chunk), 1)
    dst_row = iota((4 * per_chunk, 4 * per_chunk), 0)
    spread = (src_col == 4 * (dst_row % per_chunk) + dst_row // per_chunk).astype(F32).astype(BF16)

    def arrange(sec):
        def body(i, carry):
            base = pl.multiple_of(i * 4 * per_chunk, 4 * per_chunk)
            moved = jnp.dot(spread, w4[sec, pl.ds(base, 4 * per_chunk), :], preferred_element_type=F32)
            moved = moved.astype(BF16)
            to = pl.multiple_of(i * per_chunk, per_chunk)
            for c in range(4):
                wp[sec, pl.ds(to, per_chunk), c * HD : (c + 1) * HD] = moved[
                    c * per_chunk : (c + 1) * per_chunk
                ]
            return carry

        lax.fori_loop(0, D // per_chunk, body, 0, unroll=True)

    arrange(p)
    loads[0].wait()
    loads[3].wait()
    crossed = lax.rem(yg + 2, YN)
    for pair in ((0, 5), (1, 4), (2, 3)):
        columns = []
        for j in pair:
            drain(reqin.at[peers_at(j)], req_r.at[j])
            asked = jnp.broadcast_to(reqin[peers_at(j)], (YN, 24, HD))
            on = iota((YN, 24, HD), 1) == iota((YN, 24, HD), 2)
            found = jnp.sum(jnp.where(on, asked.astype(F32), 0.0), axis=2, keepdims=True)
            columns.append(found[:, :SLOTS].reshape(YN * SLOTS, 1))
        column = jnp.concatenate(columns, axis=0)
        size = 2 * YN * SLOTS
        hot = (column == iota((size, D), 1).astype(F32)).astype(F32).astype(BF16)
        rows = jnp.dot(hot, tcol[...], preferred_element_type=F32)
        group = (iota((size, HD), 0) // SLOTS) % YN
        rows = jnp.where(group == crossed, rows[:, HD:], rows[:, :HD]).astype(BF16)
        rows = rows.reshape(2, YN, SLOTS // 2, 2, HD)
        for i, j in enumerate(pair):
            repout[peers_at(j)] = rows[i]
        to_peers(repout, repin, rep_s, rep_r, pair[::-1])

    key_col = to_column(key)
    for h in range(2):
        lanes = iota((ROWS, PEERS * SLOTS), 1).astype(F32)
        pick[h] = (key_col[h * ROWS : (h + 1) * ROWS] == lanes).astype(F32).astype(BF16)

    exchange[0].wait_recv()
    exchange[1].wait_recv()
    exchange[2].wait_recv()
    arrange(q)
    small[3].wait()
    small[4].wait()
    seg = seg_ref[pl.ds(p, 1), :].astype(F32)
    seg_col = to_column(seg)
    below = iota((ROWS, ROWS), 1) <= iota((ROWS, ROWS), 0)
    same = seg_col == jnp.broadcast_to(seg, (ROWS, ROWS))
    mask[...] = jnp.where(below & same, 1.0 / ROWS, 0.0)
    hits = jnp.zeros((ROWS, ROWS), F32)
    near = nbr_ref[p]
    for n in range(NBR):
        row = jnp.broadcast_to(near[n : n + 1], (ROWS, ROWS))
        hits = hits + jnp.where(row == iota((ROWS, ROWS), 0), 1.0 / NBR, 0.0)
    counts[...] = hits.T.astype(BF16)
    keep.wait()

    for j in range(ZN // 2):
        drain(repin.at[peers_at(j)], rep_r.at[j])
    def to_group(src_of, dst, s_sem, r_of):
        for d in (4, 2, 6, 5, 7, 1, 3):
            to = mp_peer(d)
            remote(src_of(to), dst, s_sem, r_of, (g, to, p)).start()

    halves = [slice(0, HALF), slice(HALF, ROWS)]
    rows = repin[...].reshape(PEERS * SLOTS, HD)
    swaps = []
    for h in range(2):
        theirs = jnp.dot(pick[q, halves[h]], rows, preferred_element_type=F32)
        part0[h] = theirs.astype(BF16)
        swaps.append(remote(part0.at[h], partin.at[h], xp_s.at[h], xp_r.at[h], sibling))
        swaps[h].start()
    mine = [
        jnp.dot(pick[p, halves[h]], rows, preferred_element_type=F32).astype(BF16)
        for h in range(2)
    ]
    for h in range(2):
        swaps[h].wait_recv()
        xcols[h, m] = mine[h] + partin[h]
        to_group(lambda to: xcols.at[h, m], xcols.at[h, m], ag_s.at[0], ag_r.at[0, h])

    row_start = m - m % 4
    m_across = row_start + lax.rem(m + 2, 4)
    m_beside = (row_start + lax.rem(m + 1, 4), row_start + lax.rem(m + 3, 4))

    def pass_states(src, to):
        rows_of = states.at[0, src]
        remote(rows_of, rows_of, ag_s.at[2], fin_r.at[src], (g, to, p)).start()

    own_row = pl.multiple_of(m * OWN, OWN)
    for sec in range(2):
        for h in range(2):
            if sec == 0:
                drain(xcols.at[h, pl.ds(0, MP - 1)], ag_r.at[0, h])
                total = jnp.zeros((HALF, 1), F32)
                for k in range(MP):
                    block = xcols[h, k].astype(F32)
                    total = total + jnp.sum(block * block, axis=1, keepdims=True)
                inv = lax.rsqrt(total * (1.0 / D) + EPS)
                for k in range(MP):
                    scaled = xcols[h, k].astype(F32) * inv * gbuf[0, 0:1, k * HD : (k + 1) * HD]
                    nrm[0, h, :, :, k * HD : (k + 1) * HD] = scaled.astype(BF16).reshape(MP, OWN, HD)
                    xrow[h, :, k * HD : (k + 1) * HD] = xcols[h, k, pl.ds(own_row, OWN), :].astype(F32)
            else:
                drain(nrm.at[1, h, pl.ds(0, MP - 1)], ag_r.at[1, h])
            proj = jnp.dot(nrm[sec, h].reshape(HALF, D), wp[sec], preferred_element_type=F32)
            proj = silu(proj).astype(BF16)
            rows = slice(h * HALF, (h + 1) * HALF)
            seen = slice(0, (h + 1) * HALF)
            feats[rows] = proj
            gate, query = proj[:, :HD], proj[:, 2 * HD : 3 * HD]
            scores = lax.dot_general(
                query, feats[seen, 3 * HD :], (((1,), (1,)), ((), ())), preferred_element_type=F32
            ) * HD ** (-0.5)
            attn = (silu(scores) * mask[rows, seen]).astype(BF16)
            mixed = jnp.dot(attn, feats[seen, HD : 2 * HD], preferred_element_type=F32)
            mixed = mixed * lax.rsqrt(jnp.mean(mixed * mixed, axis=1, keepdims=True) + EPS)
            gated = (mixed * gate.astype(F32)).astype(BF16)
            back = jnp.dot(gated, wo[sec], preferred_element_type=F32).astype(BF16)
            part[sec, h] = back.reshape(MP, OWN, D)
            to_group(
                lambda to: part.at[sec, h, to], rsin.at[sec, h, m], rs_s.at[sec], rs_r.at[sec, h, m]
            )
        for h in range(2):
            acc = xrow[h] + part[sec, h, m].astype(F32)
            for d in (1, 3, 5, 7, 2, 6, 4):
                src = mp_peer(d)
                drain(rsin.at[sec, h, src], rs_r.at[sec, h, src])
                acc = acc + rsin[sec, h, src].astype(F32)
            new = acc.astype(BF16)
            if sec == 0:
                newf = new.astype(F32)
                xrow[h] = newf
                inv = lax.rsqrt(jnp.mean(newf * newf, axis=1, keepdims=True) + EPS)
                nrm[1, h, m] = (newf * inv * gbuf[1, 0:1, :]).astype(BF16)
                to_group(lambda to: nrm.at[1, h, m], nrm.at[1, h, m], ag_s.at[1], ag_r.at[1, h])
            else:
                states[h, m] = new
                if h == 1:
                    to_group(lambda to: states.at[1, m], states.at[1, m], ag_s.at[2], ag_r.at[2, 1])
                else:
                    for to in (m_across, m_y) + m_beside:
                        pass_states(m, to)

    drain(states.at[0, m_y], fin_r.at[m_y])
    for to in m_beside:
        pass_states(m_y, to)
    drain(states.at[0, m_across], fin_r.at[m_across])
    pass_states(m_across, m_y)
    for src in m_beside:
        drain(states.at[0, src], fin_r.at[src])
    for src in m_beside + (m_across,):
        turned = lax.rem(src + MP // 2, MP)
        drain(states.at[0, turned], fin_r.at[turned])
    scored[...] = jnp.dot(
        states[0].reshape(HALF, D), wctx[...], preferred_element_type=F32
    ).astype(BF16)
    drain(states.at[1, pl.ds(0, MP - 1)], ag_r.at[2, 1])

    for copy in exchange:
        copy.wait_send()
    for swap in swaps:
        swap.wait_send()

    @pl.when(is_even)
    def _():
        drain(reqout.at[pl.ds(0, PEERS - 1)], req_s)
        drain(repout.at[pl.ds(0, PEERS - 1)], rep_s)

    @pl.when(p == 1)
    def _():
        drain(reqout, req_s)
        drain(repout, rep_s)

    for h in range(2):
        drain(xcols.at[h, pl.ds(0, MP - 1)], ag_s.at[0])
        drain(nrm.at[1, h, pl.ds(0, MP - 1)], ag_s.at[1])
        drain(states.at[h, pl.ds(0, MP - 1)], ag_s.at[2])
        for sec in range(2):
            drain(part.at[sec, h, pl.ds(0, MP - 1)], rs_s.at[sec])


def finish(
    states_ref, counts_ref, wctx_ref, scored_ref, bias_ref, out_hbm, ctx_hbm, ctx_ref, sem
):
    writes = [
        pltpu.make_async_copy(states_ref.at[h], out_hbm.at[h], sem.at[h]) for h in range(2)
    ]
    for write in writes:
        write.start()
    rest = jnp.dot(
        states_ref[1].reshape(HALF, D), wctx_ref[...], preferred_element_type=F32
    ).astype(BF16)
    summed = jnp.dot(counts_ref[:, :HALF], scored_ref[...], preferred_element_type=F32)
    summed = summed + jnp.dot(counts_ref[:, HALF:], rest, preferred_element_type=F32)
    ctx_ref[...] = silu(summed + bias_ref[...].astype(F32)).astype(BF16)
    writes.append(pltpu.make_async_copy(ctx_ref, ctx_hbm, sem.at[2]))
    writes[2].start()
    for write in writes:
        write.wait()


def on_device(
    item_owner, item_row, segments, neighbors, table, gains, w_in, w_out, w_ctx, ctx_bias
):
    n_rows = item_row.shape[0]
    vmem = pl.BlockSpec(memory_space=pltpu.VMEM)
    hbm = pl.BlockSpec(memory_space=pltpu.HBM)
    dma = pltpu.SemaphoreType.DMA
    states, counts, wctx, scored = pl.pallas_call(
        kernel,
        out_shape=(
            pltpu.VMEM((2, MP, OWN, D), BF16),
            pltpu.VMEM((ROWS, ROWS), BF16),
            pltpu.VMEM((D, HD), BF16),
            pltpu.VMEM((HALF, HD), BF16),
        ),
        in_specs=[hbm] * 9,
        out_specs=(vmem, vmem, vmem, vmem),
        scratch_shapes=[
            pltpu.VMEM((1, n_rows), I32),
            pltpu.VMEM((1, n_rows), I32),
            pltpu.VMEM((2, ROWS), I32),
            pltpu.VMEM((2, NBR, ROWS), I32),
            pltpu.VMEM((1, D), BF16),
            pltpu.VMEM((D, 2 * HD), BF16),
            pltpu.VMEM((2, 4 * D, HD), BF16),
            pltpu.VMEM((2, D, 4 * HD), BF16),
            pltpu.VMEM((2, HD, D), BF16),
            pltpu.VMEM((2, 8, D), F32),
            pltpu.VMEM((PEERS, 1, HD), I32),
            pltpu.VMEM((PEERS, 1, HD), I32),
            pltpu.VMEM((PEERS, SLOTS // 2, 2, HD), BF16),
            pltpu.VMEM((PEERS, SLOTS // 2, 2, HD), BF16),
            pltpu.VMEM((2, ROWS, PEERS * SLOTS), BF16),
            pltpu.VMEM((2, HALF, HD), BF16),
            pltpu.VMEM((2, HALF, HD), BF16),
            pltpu.VMEM((2, MP, HALF, HD), BF16),
            pltpu.VMEM((ROWS, ROWS), F32),
            pltpu.VMEM((2, 2, MP, OWN, D), BF16),
            pltpu.VMEM((ROWS, 4 * HD), BF16),
            pltpu.VMEM((2, 2, MP, OWN, D), BF16),
            pltpu.VMEM((2, 2, MP, OWN, D), BF16),
            pltpu.VMEM((2, OWN, D), F32),
            dma((10,)),
            dma(()),
            dma((ZN // 2,)),
            dma(()),
            dma((ZN // 2,)),
            dma((3,)),
            dma((3,)),
            dma((2,)),
            dma((2,)),
            dma((3,)),
            dma((3, 2)),
            dma((2,)),
            dma((2, 2, MP)),
            dma((MP,)),
        ],
        compiler_params=pltpu.CompilerParams(
            collective_id=0, has_side_effects=True, vmem_limit_bytes=65700000
        ),
        name="cascade",
    )(
        item_owner.reshape(1, n_rows),
        item_row.reshape(1, n_rows),
        segments[0],
        jnp.swapaxes(neighbors[0], 1, 2),
        gains,
        table,
        w_in.reshape(4 * D, HD),
        w_out[0],
        w_ctx,
    )
    states, ctx = pl.pallas_call(
        finish,
        out_shape=(
            jax.ShapeDtypeStruct((2, MP, OWN, D), BF16),
            jax.ShapeDtypeStruct((ROWS, HD), BF16),
        ),
        in_specs=[vmem] * 5,
        out_specs=(hbm, hbm),
        scratch_shapes=[pltpu.VMEM((ROWS, HD), BF16), dma((3,))],
        compiler_params=pltpu.CompilerParams(vmem_limit_bytes=8 * 1024 * 1024),
        name="finish",
    )(states, counts, wctx, scored, ctx_bias.reshape(1, -1))
    return states.reshape(1, 1, ROWS, D), ctx.reshape(1, 1, ROWS, HD)


def solution(mesh):
    in_specs = (
        P("dp", None),
        P("dp"),
        P("dp", None, None),
        P("dp", None, None, None),
        P("dp", None),
        P("phase", None),
        P("phase", None, None, "mp"),
        P("phase", "mp", None),
        P(None, "mp"),
        P("mp"),
    )
    out_specs = (P("dp", "phase", None, None), P("dp", "phase", None, "mp"))
    return jax.shard_map(
        on_device, mesh=mesh, in_specs=in_specs, out_specs=out_specs, check_vma=False
    )
```
